32 devices in a mesh: pole: 2 (over x), row: 16 (over z, y, core).
Axes of the slice: x: 2, y: 2, z: 4, core: 2. Of those that a mesh axis runs over, the one named last changes fastest.
Arguments:
- anc_band: bfloat16 [32, 3, 512, 512], P(('pole', 'row')), parts along dimension 0, may hold values from -6 to 6
- panel_one: bfloat16 [32, 3, 512, 512], P(('pole', 'row')), parts along dimension 0, may hold values from -0.15625 to 0.15625
- mask_one: int32 [32, 3], P(('pole', 'row')), parts along dimension 0, may hold values 0 or 1
- dinv_one: bfloat16 [32, 512, 512], P(('pole', 'row')), parts along dimension 0, may hold values from -6 to 6
- panel_two: bfloat16 [32, 3, 512, 512], P(('pole', 'row')), parts along dimension 0, may hold values from -0.125 to 0.125
- mask_two: int32 [32, 3], P(('pole', 'row')), parts along dimension 0, may hold values 0 or 1
- par_two: bfloat16 [32, 512, 512], P(('pole', 'row')), parts along dimension 0, may hold values from -0.125 to 0.125
- dinv_two: bfloat16 [32, 512, 512], P(('pole', 'row')), parts along dimension 0, may hold values from -6 to 6
Outputs:
- inv_one: bfloat16 [32, 3, 512, 512], P(('pole', 'row')), parts along dimension 0
- diag_one: bfloat16 [32, 512, 512], P(('pole', 'row')), parts along dimension 0
- inv_two: bfloat16 [32, 3, 512, 512], P(('pole', 'row')), parts along dimension 0
- cross_two: bfloat16 [32, 512, 512], P(('pole', 'row')), parts along dimension 0
- diag_two: bfloat16 [32, 512, 512], P(('pole', 'row')), parts along dimension 0
The draws below stay inside these ranges and needn't reach their ends.
There are 2 independent parts, one for each index of `pole`. The reference program is written for one: setup_inputs(seed, part) draws one part's arguments, and reference() takes and returns one part's arrays. A program takes and returns all parts, laid end to end along the dimension named above; each array names one. Nothing has to cross between parts.
All inputs are finite; a program needn't handle non-finite values. No bound on the sum of `mask_one` or of `mask_two` on one device may be relied on, other than what follows from the above.
Results may differ from the reference program's by a relative error of at most 0.0052.
Values may be sent and summed in bfloat16 or wider, within the bound.
A program may use at most 64 MiB of HBM per device.

```python
import jax
import jax.numpy as jnp

B = 512
W = 3
NS = 16


def with_ends(array, key, least, high):
    shape = array.shape
    spot = [jax.random.randint(jax.random.fold_in(key, axis), (), 0, shape[axis]) for axis in range(len(shape))]
    array = array.at[tuple(spot)].set(least)
    longest = shape.index(max(shape))
    spot[longest] = (spot[longest] + 1) % shape[longest]
    return array.at[tuple(spot)].set(high)


def block_scale(own_key, extent, cuts, least, top_value):
    def one(position, blocks):
        draws = jax.random.uniform(jax.random.fold_in(jax.random.fold_in(own_key, 6), position), (blocks,), jnp.float32, least / len(cuts), top_value / len(cuts))
        return jnp.repeat(jnp.exp(draws), extent[position] // blocks).reshape((-1,) + (1,) * (len(extent) - position - 1))

    factor_of = one(*cuts[0])
    for cut in cuts[1:]:
        factor_of = factor_of * one(*cut)
    return factor_of


def scatter_about(own_key, shape, spread, bound, pieces=(), held_as=jnp.bfloat16):
    entries = jax.random.normal(own_key, shape, jnp.float32) * spread
    if len(pieces) > 0:
        entries = block_scale(own_key, shape, pieces, -0.22, 0.18) * entries
    return jnp.clip(entries, min=-bound, max=bound).astype(held_as)


def setup_inputs(seed: int = 0, part: int = 0) -> dict:
    streams_of = jax.random.split(jax.random.key(seed), 9)
    part_splits = jax.random.split(jax.random.fold_in(streams_of[8], part), 9)
    return {
        "anc_band": scatter_about(part_splits[0], (NS, W, B, B), 1.0, 6.0, ((0, 16),)),
        "panel_one": scatter_about(part_splits[1], (NS, W, B, B), (3 * B) ** -0.5, 0.15625, ((0, 16),)),
        "mask_one": with_ends((jax.random.randint(part_splits[2], (NS, W), 0, 4) < 3).astype(jnp.int32), jax.random.fold_in(part_splits[2], 1), 0, 1),
        "dinv_one": scatter_about(part_splits[3], (NS, B, B), 1.0, 6.0, ((0, 16),)),
        "panel_two": scatter_about(part_splits[4], (NS, W, B, B), (4 * B) ** -0.5, 0.125, ((0, 16),)),
        "mask_two": with_ends((jax.random.randint(part_splits[5], (NS, W), 0, 4) < 3).astype(jnp.int32), jax.random.fold_in(part_splits[5], 1), 0, 1),
        "par_two": scatter_about(part_splits[6], (NS, B, B), (4 * B) ** -0.5, 0.125, ((0, 16),)),
        "dinv_two": scatter_about(part_splits[7], (NS, B, B), 1.0, 6.0, ((0, 16),)),
    }


def near(values, offset):
    if offset == 0:
        return values
    return jnp.roll(values, offset, 0)


def product(left, right):
    return jnp.einsum("nij,njk->nik", left.astype(jnp.float32), right.astype(jnp.float32))


def turned(left, right):
    return jnp.einsum("nji,njk->nik", left.astype(jnp.float32), right.astype(jnp.float32))


def apply_band(anc_band, delta, right):
    if delta >= 0:
        return product(anc_band[:, delta], right)
    return turned(near(anc_band[:, -delta], -delta), right)


def solve_rows(anc_band, panel, flags, leading):
    width = anc_band.shape[1]
    columns = []
    for first in range(width):
        summed = leading(first)
        for second in range(width):
            offset = first - second
            weight = near(flags[:, second], offset)[:, None, None]
            summed = summed + weight * apply_band(anc_band, second - first, near(panel[:, second], offset))
        columns.append((-summed * flags[:, first][:, None, None]).astype(jnp.bfloat16))
    return jnp.stack(columns, 1)


def reference(anc_band, panel_one, mask_one, dinv_one, panel_two, mask_two, par_two, dinv_two):
    count, width, block, _ = anc_band.shape
    leading_column = (jnp.arange(width, dtype=jnp.int32) == 0)[None, :]
    flag_one = jnp.where(leading_column, 1.0, mask_one.astype(jnp.float32))
    flag_two = jnp.where(leading_column, 1.0, flag_one * mask_two.astype(jnp.float32))
    zero_block = jnp.zeros((count, block, block), jnp.float32)
    inv_one = solve_rows(anc_band, panel_one, flag_one, lambda first: zero_block)
    summed = dinv_one.astype(jnp.float32)
    for second in range(width):
        summed = summed - near(turned(panel_one[:, second], inv_one[:, second]), -second)
    diag_one = summed.astype(jnp.bfloat16)

    def parent_term(first):
        return product(inv_one[:, first], near(par_two, first))

    inv_two = solve_rows(anc_band, panel_two, flag_two, parent_term)
    summed = product(diag_one, par_two)
    for second in range(width):
        term = flag_two[:, second][:, None, None] * turned(inv_one[:, second], panel_two[:, second])
        summed = summed + near(term, -second)
    cross_two = (-summed).astype(jnp.bfloat16)
    summed = dinv_two.astype(jnp.float32) - turned(par_two, cross_two)
    for second in range(width):
        summed = summed - near(turned(panel_two[:, second], inv_two[:, second]), -second)
    diag_two = summed.astype(jnp.bfloat16)
    return inv_one, diag_one, inv_two, cross_two, diag_two
```

```python
import functools

import jax
import jax.numpy as jnp
from jax import lax
from jax.experimental import pallas as pl
from jax.experimental.pallas import tpu as pltpu
from jax.sharding import PartitionSpec as P

TILE = 256
MESH = pl.DeviceIdType.MESH


def columns(block):
    def wrap(step):
        @pl.loop(0, block // TILE)
        def _(c):
            step(pl.ds(pl.multiple_of(c * TILE, TILE), TILE))

    return wrap


def plain(left, right):
    return jnp.dot(left[...], right, preferred_element_type=jnp.float32)


def turned(left, right):
    return lax.dot_general(
        left[...], right, (((0,), (0,)), ((), ())), preferred_element_type=jnp.float32
    )


def kernel(
    count,
    mask_one, mask_two, anc, p_one, d_one, p_two, par_in, d_two,
    out,
    a, one, two, par, dinv_one, dinv_two,
    near, far, got_one, got_two, inv_one, inv_two,
    diag_one, cross, diag_two, part_one, part_two, m_one, m_two, flags, got_flags,
    load_sem, store_sem, send_sem, recv_sem,
):
    block = par.shape[0]
    me = lax.axis_index("row")
    odd = lax.rem(me, 2) == 1
    up = [None] + [lax.rem(me + q, count) for q in (1, 2)]
    down = [None] + [lax.rem(me + count - q, count) for q in (1, 2)]

    loads = [
        pltpu.make_async_copy(source, target, load_sem.at[i])
        for i, (source, target) in enumerate(
            [
                (mask_one, m_one),
                (mask_two, m_two),
                (p_one.at[0, 0], one),
                (anc.at[0], a),
                (p_two.at[0, 0], two),
                (par_in.at[0], par),
                (d_one.at[0], dinv_one),
                (d_two.at[0], dinv_two),
            ]
        )
    ]
    barrier = pltpu.get_barrier_semaphore()
    for peer in up[1:] + down[1:]:
        pl.semaphore_signal(barrier, inc=1, device_id={"row": peer}, device_id_type=MESH)
    for load in loads:
        load.start()
    pl.semaphore_wait(barrier, 4)

    def remote(source, target, send, recv, peer):
        return pltpu.make_async_remote_copy(
            src_ref=source,
            dst_ref=target,
            send_sem=send_sem.at[send],
            recv_sem=recv_sem.at[recv],
            device_id={"row": peer},
            device_id_type=MESH,
        )

    near_0 = remote(anc.at[0, 0], near.at[0], 0, 0, down[1])
    near_1 = remote(anc.at[0, 1], near.at[1], 1, 1, down[1])
    far_odd = remote(anc.at[0, 0], far, 2, 2, down[2])
    far_pass = remote(near.at[0], far, 2, 2, down[1])
    send_one = [None] + [remote(p_one.at[0, q], got_one.at[q - 1], 2 + q, 2 + q, down[q]) for q in (1, 2)]
    send_two = [None] + [remote(p_two.at[0, q], got_two.at[q - 1], 4 + q, 4 + q, down[q]) for q in (1, 2)]
    send_flags = [None] + [remote(flags, got_flags.at[q - 1], 6 + q, 6 + q, down[q]) for q in (1, 2)]
    give_one = [None] + [remote(inv_one.at[p], out.at[p], 8 + p, 8 + p, up[p]) for p in (1, 2)]
    give_two = [None] + [remote(inv_two.at[p], out.at[3 + p], 10 + p, 10 + p, up[p]) for p in (1, 2)]

    near_0.start()
    loads[0].wait()
    loads[1].wait()
    flag_one = [None] + [m_one[0, q].astype(jnp.float32) for q in (1, 2)]
    flag_two = [None] + [flag_one[q] * m_two[0, q].astype(jnp.float32) for q in (1, 2)]
    spot = lax.broadcasted_iota(jnp.int32, flags.shape, 0)
    value = jnp.where(spot == 0, flag_one[1], flag_one[2])
    value = jnp.where(spot == 2, flag_two[1], value)
    flags[...] = jnp.where(spot == 3, flag_two[2], value)
    for q in (2, 1):
        send_flags[q].start()
    send_one[2].start()
    send_one[1].start()
    near_1.start()

    @pl.when(odd)
    def _():
        far_odd.start()

    send_two[1].start()
    send_two[2].start()

    def kept(p, level):
        return got_flags[p - 1, pl.ds(2 * level + p - 1, 1), 0:1]

    def masked(ref, q, level):
        flag = kept(q, level).astype(ref.dtype)

        @pl.loop(0, block // 64)
        def _(r):
            rows = pl.ds(pl.multiple_of(r * 64, 64), 64)
            ref[rows, :] = ref[rows, :] * flag

    for load in loads[2:]:
        load.wait()

    @columns(block)
    def _(c):
        for part, own in ((part_one, one), (part_two, two)):
            part[0, :, c] = plain(a.at[0], own[:, c])
            for p in (1, 2):
                part[p, :, c] = turned(a.at[p], own[:, c])

    near_0.wait_recv()

    @pl.when(jnp.logical_not(odd))
    def _():
        far_odd.wait_recv()

    @pl.when(odd)
    def _():
        far_odd.wait_send()
        far_pass.start()

    for q in (1, 2):
        send_flags[q].wait_recv()

    for q in (1, 2):
        send_one[q].wait_recv()
        masked(got_one.at[q - 1], q, 0)

    def solve(p, c, got, total):
        first, second = got[0, :, c], got[1, :, c]
        if p == 0:
            return total + plain(a.at[1], first) + plain(a.at[2], second)
        if p == 1:
            return total + plain(near.at[0], first) + plain(near.at[1], second)
        return total + turned(near.at[1], first) + plain(far, second)

    def negated(p, level, total):
        return -total * kept(p, level) if p else -total

    near_1.wait_recv()

    @pl.when(odd)
    def _():
        far_odd.wait_recv()

    for p in (2, 1, 0):
        @columns(block)
        def _(c):
            total = solve(p, c, got_one, part_one[p, :, c])
            inv_one[p, :, c] = negated(p, 0, total).astype(jnp.bfloat16)

        if p:
            give_one[p].start()

    stores = []

    def store(source, target):
        stores.append(pltpu.make_async_copy(source, target, store_sem.at[len(stores)]))
        stores[-1].start()

    store(inv_one.at[0], out.at[0])

    for p in (2, 1, 0):
        @columns(block)
        def _(c):
            part_two[p, :, c] += plain(inv_one.at[p], par[:, c])

    for q in (1, 2):
        send_two[q].wait_recv()
        masked(got_two.at[q - 1], q, 1)
    for p in (2, 1, 0):
        @columns(block)
        def _(c):
            total = solve(p, c, got_two, part_two[p, :, c])
            inv_two[p, :, c] = negated(p, 1, total).astype(jnp.bfloat16)

        if p:
            give_two[p].start()

    store(inv_two.at[0], out.at[3])

    @columns(block)
    def _(c):
        total = dinv_one[:, c].astype(jnp.float32) - turned(one, inv_one[0, :, c])
        for q in (1, 2):
            total = total - turned(got_one.at[q - 1], inv_one[q, :, c])
        diag_one[:, c] = total.astype(jnp.bfloat16)

    store(diag_one, out.at[6])

    @columns(block)
    def _(c):
        total = plain(diag_one, par[:, c]) + turned(inv_one.at[0], two[:, c])
        for q in (1, 2):
            total = total + turned(inv_one.at[q], got_two[q - 1, :, c])
        cross[:, c] = (-total).astype(jnp.bfloat16)

    store(cross, out.at[7])

    @columns(block)
    def _(c):
        total = dinv_two[:, c].astype(jnp.float32) - turned(par, cross[:, c])
        total = total - turned(two, inv_two[0, :, c])
        for q in (1, 2):
            total = total - turned(got_two.at[q - 1], inv_two[q, :, c])
        diag_two[:, c] = total.astype(jnp.bfloat16)

    store(diag_two, out.at[8])

    for copy in (near_0, near_1):
        copy.wait_send()

    @pl.when(odd)
    def _():
        far_pass.wait_send()

    for group in (send_flags, send_one, send_two, give_one, give_two):
        for q in (1, 2):
            group[q].wait_send()
    for item in stores:
        item.wait()
    for give in (give_one, give_two):
        for p in (1, 2):
            give[p].wait_recv()


def place(held, o_inv_one, o_diag_one, o_inv_two, o_cross, o_diag_two, sem):
    copies = [
        pltpu.make_async_copy(source, target, sem.at[i])
        for i, (source, target) in enumerate(
            [
                (held.at[pl.ds(0, 3)], o_inv_one.at[0]),
                (held.at[pl.ds(3, 3)], o_inv_two.at[0]),
                (held.at[6], o_diag_one.at[0]),
                (held.at[7], o_cross.at[0]),
                (held.at[8], o_diag_two.at[0]),
            ]
        )
    ]
    for copy in copies:
        copy.start()
    for copy in copies:
        copy.wait()


def body(anc_band, panel_one, mask_one, dinv_one, panel_two, mask_two, par_two, dinv_two):
    block = anc_band.shape[2]
    kind = anc_band.dtype

    def blocks(number, dtype=kind):
        lead = () if number is None else (number,)
        return pltpu.VMEM(lead + (block, block), dtype)

    hbm = pl.BlockSpec(memory_space=pltpu.HBM)
    free = pl.BlockSpec(memory_space=pl.ANY)
    count = lax.axis_size("row")
    held = pl.pallas_call(
        functools.partial(kernel, count),
        out_shape=pltpu.VMEM((9, block, block), kind),
        in_specs=[hbm] * 8,
        out_specs=free,
        scratch_shapes=[
            blocks(3), blocks(None), blocks(None), blocks(None), blocks(None), blocks(None),
            blocks(2), blocks(None), blocks(2), blocks(2), blocks(3), blocks(3),
            blocks(None), blocks(None), blocks(None), blocks(3, jnp.float32), blocks(3, jnp.float32),
            pltpu.SMEM(mask_one.shape, jnp.int32), pltpu.SMEM(mask_two.shape, jnp.int32),
            pltpu.VMEM((8, 128), jnp.float32), pltpu.VMEM((2, 8, 128), jnp.float32),
            pltpu.SemaphoreType.DMA((8,)),
            pltpu.SemaphoreType.DMA((5,)),
            pltpu.SemaphoreType.DMA((13,)),
            pltpu.SemaphoreType.DMA((13,)),
        ],
        compiler_params=pltpu.CompilerParams(
            collective_id=0, has_side_effects=True, vmem_limit_bytes=40 * 2**20
        ),
    )(*(
        pltpu.with_memory_space_constraint(x, pltpu.HBM)
        for x in (mask_one, mask_two, anc_band, panel_one, dinv_one, panel_two, par_two, dinv_two)
    ))
    return pl.pallas_call(
        place,
        out_shape=[
            jax.ShapeDtypeStruct(anc_band.shape, kind),
            jax.ShapeDtypeStruct(dinv_one.shape, kind),
            jax.ShapeDtypeStruct(anc_band.shape, kind),
            jax.ShapeDtypeStruct(dinv_one.shape, kind),
            jax.ShapeDtypeStruct(dinv_one.shape, kind),
        ],
        in_specs=[free],
        out_specs=[hbm] * 5,
        scratch_shapes=[pltpu.SemaphoreType.DMA((5,))],
        compiler_params=pltpu.CompilerParams(vmem_limit_bytes=2**20),
    )(held)


def solution(mesh):
    four = P(("pole", "row"), None, None, None)
    three = P(("pole", "row"), None, None)
    two = P(("pole", "row"), None)
    return jax.shard_map(
        body,
        mesh=mesh,
        in_specs=(four, four, two, three, four, two, three, three),
        out_specs=(four, three, four, three, three),
        check_vma=False,
    )
```

```python
import functools

import jax
import jax.numpy as jnp
from jax import lax
from jax.experimental import pallas as pl
from jax.experimental.pallas import tpu as pltpu
from jax.sharding import PartitionSpec as P

TILE = 256
MESH = pl.DeviceIdType.MESH


def columns(block):
    def wrap(step):
        @pl.loop(0, block // TILE)
        def _(c):
            step(pl.ds(pl.multiple_of(c * TILE, TILE), TILE))

    return wrap


def plain(left, right):
    return jnp.dot(left[...], right, preferred_element_type=jnp.float32)


def turned(left, right):
    return lax.dot_general(
        left[...], right, (((0,), (0,)), ((), ())), preferred_element_type=jnp.float32
    )


def kernel(
    count,
    mask_one, mask_two, anc, p_one, d_one, p_two, par_in, d_two,
    out,
    a, one, two, par, dinv_one, dinv_two,
    near, far, got_one, got_two, inv_one, inv_two,
    diag_one, cross, diag_two, part_one, part_two, m_one, m_two, flags, got_flags,
    load_sem, store_sem, send_sem, recv_sem,
):
    block = par.shape[0]
    me = lax.axis_index("row")
    odd = lax.rem(me, 2) == 1
    up = [None] + [lax.rem(me + q, count) for q in (1, 2)]
    down = [None] + [lax.rem(me + count - q, count) for q in (1, 2)]

    loads = [
        pltpu.make_async_copy(source, target, load_sem.at[i])
        for i, (source, target) in enumerate(
            [
                (mask_one, m_one),
                (mask_two, m_two),
                (p_one.at[0, 0], one),
                (anc.at[0], a),
                (p_two.at[0, 0], two),
                (par_in.at[0], par),
                (d_one.at[0], dinv_one),
                (d_two.at[0], dinv_two),
            ]
        )
    ]
    barrier = pltpu.get_barrier_semaphore()
    for peer in up[1:] + down[1:]:
        pl.semaphore_signal(barrier, inc=1, device_id={"row": peer}, device_id_type=MESH)
    for load in loads:
        load.start()
    pl.semaphore_wait(barrier, 4)

    def remote(source, target, send, recv, peer):
        return pltpu.make_async_remote_copy(
            src_ref=source,
            dst_ref=target,
            send_sem=send_sem.at[send],
            recv_sem=recv_sem.at[recv],
            device_id={"row": peer},
            device_id_type=MESH,
        )

    near_0 = remote(anc.at[0, 0], near.at[0], 0, 0, down[1])
    near_1 = remote(anc.at[0, 1], near.at[1], 1, 1, down[1])
    far_odd = remote(anc.at[0, 0], far, 2, 2, down[2])
    far_pass = remote(near.at[0], far, 7, 2, down[1])
    send_one = [None] + [remote(p_one.at[0, q], got_one.at[q - 1], 2 + q, 2 + q, down[q]) for q in (1, 2)]
    send_two = [None] + [remote(p_two.at[0, q], got_two.at[q - 1], 4 + q, 4 + q, down[q]) for q in (1, 2)]
    send_flags = [None] + [remote(flags, got_flags.at[q - 1], 7 + q, 6 + q, down[q]) for q in (1, 2)]
    give_one = [None] + [remote(inv_one.at[p], out.at[p], 9 + p, 8 + p, up[p]) for p in (1, 2)]
    give_two = [None] + [remote(inv_two.at[p], out.at[3 + p], 11 + p, 10 + p, up[p]) for p in (1, 2)]

    near_0.start()
    loads[0].wait()
    loads[1].wait()
    flag_one = [None] + [m_one[0, q].astype(jnp.float32) for q in (1, 2)]
    flag_two = [None] + [flag_one[q] * m_two[0, q].astype(jnp.float32) for q in (1, 2)]
    spot = lax.broadcasted_iota(jnp.int32, flags.shape, 0)
    value = jnp.where(spot == 0, flag_one[1], flag_one[2])
    value = jnp.where(spot == 2, flag_two[1], value)
    flags[...] = jnp.where(spot == 3, flag_two[2], value)
    for q in (2, 1):
        send_flags[q].start()
    send_one[2].start()
    send_one[1].start()
    near_1.start()

    @pl.when(odd)
    def _():
        far_odd.start()

    send_two[2].start()
    send_two[1].start()

    def kept(p, level):
        return got_flags[p - 1, pl.ds(2 * level + p - 1, 1), 0:1]

    def masked(ref, q, level):
        flag = kept(q, level).astype(ref.dtype)

        @pl.loop(0, block // 64)
        def _(r):
            rows = pl.ds(pl.multiple_of(r * 64, 64), 64)
            ref[rows, :] = ref[rows, :] * flag

    for load in loads[2:]:
        load.wait()

    @columns(block)
    def _(c):
        for part, own in ((part_one, one), (part_two, two)):
            part[0, :, c] = plain(a.at[0], own[:, c])
            for p in (1, 2):
                part[p, :, c] = turned(a.at[p], own[:, c])

    near_0.wait_recv()

    @pl.when(jnp.logical_not(odd))
    def _():
        far_odd.wait_recv()

    @pl.when(odd)
    def _():
        far_pass.start()

    for q in (1, 2):
        send_flags[q].wait_recv()

    for q in (1, 2):
        send_one[q].wait_recv()
        masked(got_one.at[q - 1], q, 0)

    def solve(p, c, got, total):
        first, second = got[0, :, c], got[1, :, c]
        if p == 0:
            return total + plain(a.at[1], first) + plain(a.at[2], second)
        if p == 1:
            return total + plain(near.at[0], first) + plain(near.at[1], second)
        return total + turned(near.at[1], first) + plain(far, second)

    def negated(p, level, total):
        return -total * kept(p, level) if p else -total

    near_1.wait_recv()

    @pl.when(odd)
    def _():
        far_odd.wait_recv()

    for p in (2, 1, 0):
        @columns(block)
        def _(c):
            total = solve(p, c, got_one, part_one[p, :, c])
            inv_one[p, :, c] = negated(p, 0, total).astype(jnp.bfloat16)

    stores = []

    def store(source, target):
        stores.append(pltpu.make_async_copy(source, target, store_sem.at[len(stores)]))
        stores[-1].start()

    store(inv_one.at[0], out.at[0])

    for p in (2, 1, 0):
        @columns(block)
        def _(c):
            part_two[p, :, c] += plain(inv_one.at[p], par[:, c])

    @columns(block)
    def _(c):
        total = dinv_one[:, c].astype(jnp.float32) - turned(one, inv_one[0, :, c])
        for q in (1, 2):
            total = total - turned(got_one.at[q - 1], inv_one[q, :, c])
        diag_one[:, c] = total.astype(jnp.bfloat16)

    store(diag_one, out.at[6])

    send_two[2].wait_recv()
    masked(got_two.at[1], 2, 1)

    send_two[1].wait_recv()
    for copy in (near_0, near_1, send_one[1], send_one[2], send_two[1], send_two[2]):
        copy.wait_send()

    @pl.when(odd)
    def _():
        far_odd.wait_send()

    for p in (2, 1):
        give_one[p].start()

    masked(got_two.at[0], 1, 1)
    for p in (2, 1, 0):
        @columns(block)
        def _(c):
            total = solve(p, c, got_two, part_two[p, :, c])
            inv_two[p, :, c] = negated(p, 1, total).astype(jnp.bfloat16)

        if p:
            give_two[p].start()

    store(inv_two.at[0], out.at[3])

    @columns(block)
    def _(c):
        total = plain(diag_one, par[:, c]) + turned(inv_one.at[0], two[:, c])
        for q in (1, 2):
            total = total + turned(inv_one.at[q], got_two[q - 1, :, c])
        cross[:, c] = (-total).astype(jnp.bfloat16)

    store(cross, out.at[7])

    @columns(block)
    def _(c):
        total = dinv_two[:, c].astype(jnp.float32) - turned(par, cross[:, c])
        total = total - turned(two, inv_two[0, :, c])
        for q in (1, 2):
            total = total - turned(got_two.at[q - 1], inv_two[q, :, c])
        diag_two[:, c] = total.astype(jnp.bfloat16)

    store(diag_two, out.at[8])

    @pl.when(odd)
    def _():
        far_pass.wait_send()

    for group in (send_flags, give_one, give_two):
        for q in (1, 2):
            group[q].wait_send()
    for item in stores:
        item.wait()
    for give in (give_one, give_two):
        for p in (1, 2):
            give[p].wait_recv()


def place(held, o_inv_one, o_diag_one, o_inv_two, o_cross, o_diag_two, sem):
    copies = [
        pltpu.make_async_copy(source, target, sem.at[i])
        for i, (source, target) in enumerate(
            [
                (held.at[pl.ds(0, 3)], o_inv_one.at[0]),
                (held.at[pl.ds(3, 3)], o_inv_two.at[0]),
                (held.at[6], o_diag_one.at[0]),
                (held.at[7], o_cross.at[0]),
                (held.at[8], o_diag_two.at[0]),
            ]
        )
    ]
    for copy in copies:
        copy.start()
    for copy in copies:
        copy.wait()


def body(anc_band, panel_one, mask_one, dinv_one, panel_two, mask_two, par_two, dinv_two):
    block = anc_band.shape[2]
    kind = anc_band.dtype

    def blocks(number, dtype=kind):
        lead = () if number is None else (number,)
        return pltpu.VMEM(lead + (block, block), dtype)

    hbm = pl.BlockSpec(memory_space=pltpu.HBM)
    free = pl.BlockSpec(memory_space=pl.ANY)
    count = lax.axis_size("row")
    held = pl.pallas_call(
        functools.partial(kernel, count),
        out_shape=pltpu.VMEM((9, block, block), kind),
        in_specs=[hbm] * 8,
        out_specs=free,
        scratch_shapes=[
            blocks(3), blocks(None), blocks(None), blocks(None), blocks(None), blocks(None),
            blocks(2), blocks(None), blocks(2), blocks(2), blocks(3), blocks(3),
            blocks(None), blocks(None), blocks(None), blocks(3, jnp.float32), blocks(3, jnp.float32),
            pltpu.SMEM(mask_one.shape, jnp.int32), pltpu.SMEM(mask_two.shape, jnp.int32),
            pltpu.VMEM((8, 128), jnp.float32), pltpu.VMEM((2, 8, 128), jnp.float32),
            pltpu.SemaphoreType.DMA((8,)),
            pltpu.SemaphoreType.DMA((5,)),
            pltpu.SemaphoreType.DMA((14,)),
            pltpu.SemaphoreType.DMA((13,)),
        ],
        compiler_params=pltpu.CompilerParams(
            collective_id=0, has_side_effects=True, vmem_limit_bytes=40 * 2**20
        ),
    )(*(
        pltpu.with_memory_space_constraint(x, pltpu.HBM)
        for x in (mask_one, mask_two, anc_band, panel_one, dinv_one, panel_two, par_two, dinv_two)
    ))
    return pl.pallas_call(
        place,
        out_shape=[
            jax.ShapeDtypeStruct(anc_band.shape, kind),
            jax.ShapeDtypeStruct(dinv_one.shape, kind),
            jax.ShapeDtypeStruct(anc_band.shape, kind),
            jax.ShapeDtypeStruct(dinv_one.shape, kind),
            jax.ShapeDtypeStruct(dinv_one.shape, kind),
        ],
        in_specs=[free],
        out_specs=[hbm] * 5,
        scratch_shapes=[pltpu.SemaphoreType.DMA((5,))],
        compiler_params=pltpu.CompilerParams(vmem_limit_bytes=2**20),
    )(held)


def solution(mesh):
    four = P(("pole", "row"), None, None, None)
    three = P(("pole", "row"), None, None)
    two = P(("pole", "row"), None)
    return jax.shard_map(
        body,
        mesh=mesh,
        in_specs=(four, four, two, three, four, two, three, three),
        out_specs=(four, three, four, three, three),
        check_vma=False,
    )
```

```python
import functools

import jax
import jax.numpy as jnp
from jax import lax
from jax.experimental import pallas as pl
from jax.experimental.pallas import tpu as pltpu
from jax.sharding import PartitionSpec as P

TILE = 256
MESH = pl.DeviceIdType.MESH


def columns(block):
    def wrap(step):
        @pl.loop(0, block // TILE)
        def _(c):
            step(pl.ds(pl.multiple_of(c * TILE, TILE), TILE))

    return wrap


def plain(left, right):
    return jnp.dot(left[...], right, preferred_element_type=jnp.float32)


def turned(left, right):
    return lax.dot_general(
        left[...], right, (((0,), (0,)), ((), ())), preferred_element_type=jnp.float32
    )


def kernel(
    count,
    mask_one, mask_two, anc, p_one, d_one, p_two, par_in, d_two,
    out,
    a, one, two, par, dinv_one, dinv_two,
    near, far, got_one, got_two, inv_one, inv_two,
    diag_one, cross, diag_two, part_one, part_two, m_one, m_two, flags, got_flags,
    load_sem, store_sem, send_sem, recv_sem, go_sem,
):
    block = par.shape[0]
    me = lax.axis_index("row")
    odd = lax.rem(me, 2) == 1
    upper = lax.rem(me, 4) >= 2
    lower = jnp.logical_not(upper)
    last = me >= count - 2
    bounds = (0, block // 4, block // 2, block)
    pieces = [pl.ds(a, b - a) for a, b in zip(bounds, bounds[1:])]
    up = [None] + [lax.rem(me + q, count) for q in (1, 2)]
    down = [None] + [lax.rem(me + count - q, count) for q in (1, 2)]

    loads = [
        pltpu.make_async_copy(source, target, load_sem.at[i])
        for i, (source, target) in enumerate(
            [
                (mask_one, m_one),
                (mask_two, m_two),
                (p_one.at[0, 0], one),
                (anc.at[0], a),
                (p_two.at[0, 0], two),
                (par_in.at[0], par),
                (d_one.at[0], dinv_one),
                (d_two.at[0], dinv_two),
            ]
        )
    ]
    barrier = pltpu.get_barrier_semaphore()
    for peer in up[1:]:
        pl.semaphore_signal(barrier, inc=1, device_id={"row": peer}, device_id_type=MESH)
    for load in loads:
        load.start()
    pl.semaphore_wait(barrier, 2)

    def remote(source, target, send, recv, peer):
        return pltpu.make_async_remote_copy(
            src_ref=source,
            dst_ref=target,
            send_sem=send_sem.at[send],
            recv_sem=recv_sem.at[recv],
            device_id={"row": peer},
            device_id_type=MESH,
        )

    near_0 = remote(anc.at[0, 0], near.at[0], 0, 0, down[1])
    near_1 = remote(anc.at[0, 1], near.at[1], 1, 1, down[1])
    far_odd = remote(anc.at[0, 0], far, 2, 2, down[2])
    far_pass = remote(near.at[0], far, 7, 2, down[1])
    send_one = [None] + [remote(p_one.at[0, q], got_one.at[q - 1], 2 + q, 2 + q, down[q]) for q in (1, 2)]
    send_two = [None] + [remote(p_two.at[0, q], got_two.at[q - 1], 4 + q, 4 + q, down[q]) for q in (1, 2)]
    send_two = send_two[2:] + [
        remote(p_two.at[0, 1, piece], got_two.at[0, piece], 14 + i, 13 + i, down[1])
        for i, piece in enumerate(pieces)
    ]
    send_flags = [None] + [remote(flags, got_flags.at[q - 1], 7 + q, 6 + q, down[q]) for q in (1, 2)]
    give_one = [None] + [remote(inv_one.at[p], out.at[p], 9 + p, 8 + p, up[p]) for p in (1, 2)]
    give_two = [None] + [remote(inv_two.at[p], out.at[3 + p], 11 + p, 10 + p, up[p]) for p in (1, 2)]

    near_0.start()
    loads[0].wait()
    loads[1].wait()
    flag_one = [None] + [m_one[0, q].astype(jnp.float32) for q in (1, 2)]
    flag_two = [None] + [flag_one[q] * m_two[0, q].astype(jnp.float32) for q in (1, 2)]
    spot = lax.broadcasted_iota(jnp.int32, flags.shape, 0)
    value = jnp.where(spot == 0, flag_one[1], flag_one[2])
    value = jnp.where(spot == 2, flag_two[1], value)
    flags[...] = jnp.where(spot == 3, flag_two[2], value)
    for q in (2, 1):
        send_flags[q].start()
    send_one[2].start()
    send_one[1].start()
    near_1.start()

    @pl.when(odd)
    def _():
        far_odd.start()

    for copy in send_two:
        copy.start()

    def kept(p, level):
        return got_flags[p - 1, pl.ds(2 * level + p - 1, 1), 0:1]

    def masked(ref, q, level):
        flag = kept(q, level).astype(ref.dtype)

        @pl.loop(0, block // 64)
        def _(r):
            rows = pl.ds(pl.multiple_of(r * 64, 64), 64)
            ref[rows, :] = ref[rows, :] * flag

    for load in loads[2:]:
        load.wait()

    @columns(block)
    def _(c):
        for part, own in ((part_one, one), (part_two, two)):
            part[0, :, c] = plain(a.at[0], own[:, c])
            for p in (1, 2):
                part[p, :, c] = turned(a.at[p], own[:, c])

    near_0.wait_recv()

    @pl.when(jnp.logical_not(odd))
    def _():
        far_odd.wait_recv()

    @pl.when(odd)
    def _():
        far_pass.start()

    for q in (1, 2):
        send_flags[q].wait_recv()

    for q in (1, 2):
        send_one[q].wait_recv()
        masked(got_one.at[q - 1], q, 0)

    def solve(p, c, got, total):
        first, second = got[0, :, c], got[1, :, c]
        if p == 0:
            return total + plain(a.at[1], first) + plain(a.at[2], second)
        if p == 1:
            return total + plain(near.at[0], first) + plain(near.at[1], second)
        return total + turned(near.at[1], first) + plain(far, second)

    def negated(p, level, total):
        return -total * kept(p, level) if p else -total

    near_1.wait_recv()

    @pl.when(odd)
    def _():
        far_odd.wait_recv()

    for p in (2, 1, 0):
        @columns(block)
        def _(c):
            total = solve(p, c, got_one, part_one[p, :, c])
            inv_one[p, :, c] = negated(p, 0, total).astype(jnp.bfloat16)

        if p:
            @pl.when(lower | last if p == 2 else lower)
            def _():
                give_one[p].start()

    stores = []

    def store(source, target):
        stores.append(pltpu.make_async_copy(source, target, store_sem.at[len(stores)]))
        stores[-1].start()

    store(inv_one.at[0], out.at[0])

    for p in (2, 1, 0):
        @columns(block)
        def _(c):
            part_two[p, :, c] += plain(inv_one.at[p], par[:, c])

    @columns(block)
    def _(c):
        total = dinv_one[:, c].astype(jnp.float32) - turned(one, inv_one[0, :, c])
        for q in (1, 2):
            total = total - turned(got_one.at[q - 1], inv_one[q, :, c])
        diag_one[:, c] = total.astype(jnp.bfloat16)

    store(diag_one, out.at[6])

    @pl.when(upper)
    def _():
        pl.semaphore_wait(go_sem, 1)

        @pl.when(jnp.logical_not(last))
        def _():
            give_one[2].start()

        @pl.when(odd)
        def _():
            pl.semaphore_signal(go_sem, inc=1, device_id={"row": down[1]}, device_id_type=MESH)

        give_one[1].start()

    def let_go(here):
        @pl.when(here)
        def _():
            pl.semaphore_signal(go_sem, inc=1, device_id={"row": down[2]}, device_id_type=MESH)

    wrap = me == 1
    send_two[1].wait_recv()
    let_go(wrap)
    send_two[2].wait_recv()
    let_go(lower & odd & jnp.logical_not(wrap))
    send_two[0].wait_recv()
    masked(got_two.at[1], 2, 1)
    send_two[3].wait_recv()
    masked(got_two.at[0], 1, 1)
    for p in (1, 2, 0):
        @columns(block)
        def _(c):
            total = solve(p, c, got_two, part_two[p, :, c])
            inv_two[p, :, c] = negated(p, 1, total).astype(jnp.bfloat16)

        if p:
            give_two[p].start()

    store(inv_two.at[0], out.at[3])

    @columns(block)
    def _(c):
        total = plain(diag_one, par[:, c]) + turned(inv_one.at[0], two[:, c])
        for q in (1, 2):
            total = total + turned(inv_one.at[q], got_two[q - 1, :, c])
        cross[:, c] = (-total).astype(jnp.bfloat16)

    store(cross, out.at[7])

    @columns(block)
    def _(c):
        total = dinv_two[:, c].astype(jnp.float32) - turned(par, cross[:, c])
        total = total - turned(two, inv_two[0, :, c])
        for q in (1, 2):
            total = total - turned(got_two.at[q - 1], inv_two[q, :, c])
        diag_two[:, c] = total.astype(jnp.bfloat16)

    store(diag_two, out.at[8])

    @pl.when(odd)
    def _():
        far_pass.wait_send()

    @pl.when(odd)
    def _():
        far_odd.wait_send()

    for copy in [near_0, near_1] + send_two:
        copy.wait_send()
    for group in (send_flags, send_one, give_one, give_two):
        for q in (1, 2):
            group[q].wait_send()
    for item in stores:
        item.wait()
    for give in (give_one, give_two):
        for p in (1, 2):
            give[p].wait_recv()


def place(held, o_inv_one, o_diag_one, o_inv_two, o_cross, o_diag_two, sem):
    copies = [
        pltpu.make_async_copy(source, target, sem.at[i])
        for i, (source, target) in enumerate(
            [
                (held.at[pl.ds(0, 3)], o_inv_one.at[0]),
                (held.at[pl.ds(3, 3)], o_inv_two.at[0]),
                (held.at[6], o_diag_one.at[0]),
                (held.at[7], o_cross.at[0]),
                (held.at[8], o_diag_two.at[0]),
            ]
        )
    ]
    for copy in copies:
        copy.start()
    for copy in copies:
        copy.wait()


def body(anc_band, panel_one, mask_one, dinv_one, panel_two, mask_two, par_two, dinv_two):
    block = anc_band.shape[2]
    kind = anc_band.dtype

    def blocks(number, dtype=kind):
        lead = () if number is None else (number,)
        return pltpu.VMEM(lead + (block, block), dtype)

    hbm = pl.BlockSpec(memory_space=pltpu.HBM)
    free = pl.BlockSpec(memory_space=pl.ANY)
    count = lax.axis_size("row")
    held = pl.pallas_call(
        functools.partial(kernel, count),
        out_shape=pltpu.VMEM((9, block, block), kind),
        in_specs=[hbm] * 8,
        out_specs=free,
        scratch_shapes=[
            blocks(3), blocks(None), blocks(None), blocks(None), blocks(None), blocks(None),
            blocks(2), blocks(None), blocks(2), blocks(2), blocks(3), blocks(3),
            blocks(None), blocks(None), blocks(None), blocks(3, jnp.float32), blocks(3, jnp.float32),
            pltpu.SMEM(mask_one.shape, jnp.int32), pltpu.SMEM(mask_two.shape, jnp.int32),
            pltpu.VMEM((8, 128), jnp.float32), pltpu.VMEM((2, 8, 128), jnp.float32),
            pltpu.SemaphoreType.DMA((8,)),
            pltpu.SemaphoreType.DMA((5,)),
            pltpu.SemaphoreType.DMA((17,)),
            pltpu.SemaphoreType.DMA((16,)),
            pltpu.SemaphoreType.REGULAR,
        ],
        compiler_params=pltpu.CompilerParams(
            collective_id=0, has_side_effects=True, vmem_limit_bytes=40 * 2**20
        ),
    )(*(
        pltpu.with_memory_space_constraint(x, pltpu.HBM)
        for x in (mask_one, mask_two, anc_band, panel_one, dinv_one, panel_two, par_two, dinv_two)
    ))
    return pl.pallas_call(
        place,
        out_shape=[
            jax.ShapeDtypeStruct(anc_band.shape, kind),
            jax.ShapeDtypeStruct(dinv_one.shape, kind),
            jax.ShapeDtypeStruct(anc_band.shape, kind),
            jax.ShapeDtypeStruct(dinv_one.shape, kind),
            jax.ShapeDtypeStruct(dinv_one.shape, kind),
        ],
        in_specs=[free],
        out_specs=[hbm] * 5,
        scratch_shapes=[pltpu.SemaphoreType.DMA((5,))],
        compiler_params=pltpu.CompilerParams(vmem_limit_bytes=2**20),
    )(held)


def solution(mesh):
    four = P(("pole", "row"), None, None, None)
    three = P(("pole", "row"), None, None)
    two = P(("pole", "row"), None)
    return jax.shard_map(
        body,
        mesh=mesh,
        in_specs=(four, four, two, three, four, two, three, three),
        out_specs=(four, three, four, three, three),
        check_vma=False,
    )
```

```python
import functools

import jax
import jax.numpy as jnp
from jax import lax
from jax.experimental import pallas as pl
from jax.experimental.pallas import tpu as pltpu
from jax.sharding import PartitionSpec as P

TILE = 256
MESH = pl.DeviceIdType.MESH


def columns(block):
    def wrap(step):
        @pl.loop(0, block // TILE)
        def _(c):
            step(pl.ds(pl.multiple_of(c * TILE, TILE), TILE))

    return wrap


def plain(left, right):
    return jnp.dot(left[...], right, preferred_element_type=jnp.float32)


def turned(left, right):
    return lax.dot_general(
        left[...], right, (((0,), (0,)), ((), ())), preferred_element_type=jnp.float32
    )


def kernel(
    count,
    mask_one, mask_two, anc, p_one, d_one, p_two, par_in, d_two,
    out,
    a, one, two, par, dinv_one, dinv_two,
    near, far, got_one, got_two, inv_one, inv_two,
    diag_one, cross, diag_two, part_one, part_two, m_one, m_two, flags, got_flags,
    load_sem, store_sem, send_sem, recv_sem, go_sem,
):
    block = par.shape[0]
    me = lax.axis_index("row")
    odd = lax.rem(me, 2) == 1
    upper = lax.rem(me, 4) >= 2
    lower = jnp.logical_not(upper)
    last = me >= count - 2
    bounds = (0, block // 4, block * 5 // 8, block)
    pieces = [pl.ds(a, b - a) for a, b in zip(bounds, bounds[1:])]
    up = [None] + [lax.rem(me + q, count) for q in (1, 2)]
    down = [None] + [lax.rem(me + count - q, count) for q in (1, 2)]

    loads = [
        pltpu.make_async_copy(source, target, load_sem.at[i])
        for i, (source, target) in enumerate(
            [
                (mask_one, m_one),
                (mask_two, m_two),
                (p_one.at[0, 0], one),
                (anc.at[0], a),
                (p_two.at[0, 0], two),
                (par_in.at[0], par),
                (d_one.at[0], dinv_one),
                (d_two.at[0], dinv_two),
            ]
        )
    ]
    barrier = pltpu.get_barrier_semaphore()
    for peer in up[1:]:
        pl.semaphore_signal(barrier, inc=1, device_id={"row": peer}, device_id_type=MESH)
    for load in loads:
        load.start()
    pl.semaphore_wait(barrier, 2)

    def remote(source, target, send, recv, peer):
        return pltpu.make_async_remote_copy(
            src_ref=source,
            dst_ref=target,
            send_sem=send_sem.at[send],
            recv_sem=recv_sem.at[recv],
            device_id={"row": peer},
            device_id_type=MESH,
        )

    near_0 = remote(anc.at[0, 0], near.at[0], 0, 0, down[1])
    near_1 = remote(anc.at[0, 1], near.at[1], 1, 1, down[1])
    far_odd = remote(anc.at[0, 0], far, 2, 2, down[2])
    far_pass = remote(near.at[0], far, 7, 2, down[1])
    send_one = [None] + [remote(p_one.at[0, q], got_one.at[q - 1], 2 + q, 2 + q, down[q]) for q in (1, 2)]
    send_two = [None] + [remote(p_two.at[0, q], got_two.at[q - 1], 4 + q, 4 + q, down[q]) for q in (1, 2)]
    send_two = send_two[2:] + [
        remote(p_two.at[0, 1, piece], got_two.at[0, piece], 14 + i, 13 + i, down[1])
        for i, piece in enumerate(pieces)
    ]
    send_flags = [None] + [remote(flags, got_flags.at[q - 1], 7 + q, 6 + q, down[q]) for q in (1, 2)]
    give_one = [None] + [remote(inv_one.at[p], out.at[p], 9 + p, 8 + p, up[p]) for p in (1, 2)]
    give_two = [None] + [remote(inv_two.at[p], out.at[3 + p], 11 + p, 10 + p, up[p]) for p in (1, 2)]

    near_0.start()
    loads[0].wait()
    loads[1].wait()
    flag_one = [None] + [m_one[0, q].astype(jnp.float32) for q in (1, 2)]
    flag_two = [None] + [flag_one[q] * m_two[0, q].astype(jnp.float32) for q in (1, 2)]
    spot = lax.broadcasted_iota(jnp.int32, flags.shape, 0)
    value = jnp.where(spot == 0, flag_one[1], flag_one[2])
    value = jnp.where(spot == 2, flag_two[1], value)
    flags[...] = jnp.where(spot == 3, flag_two[2], value)
    for q in (2, 1):
        send_flags[q].start()
    send_one[2].start()
    send_one[1].start()
    near_1.start()

    @pl.when(odd)
    def _():
        far_odd.start()

    for copy in send_two:
        copy.start()

    def kept(p, level):
        return got_flags[p - 1, pl.ds(2 * level + p - 1, 1), 0:1]

    def masked(ref, q, level):
        flag = kept(q, level).astype(ref.dtype)

        @pl.loop(0, block // 64)
        def _(r):
            rows = pl.ds(pl.multiple_of(r * 64, 64), 64)
            ref[rows, :] = ref[rows, :] * flag

    for load in loads[2:]:
        load.wait()

    @columns(block)
    def _(c):
        for part, own in ((part_one, one), (part_two, two)):
            part[0, :, c] = plain(a.at[0], own[:, c])
            for p in (1, 2):
                part[p, :, c] = turned(a.at[p], own[:, c])

    near_0.wait_recv()

    @pl.when(jnp.logical_not(odd))
    def _():
        far_odd.wait_recv()

    @pl.when(odd)
    def _():
        far_pass.start()

    for q in (1, 2):
        send_flags[q].wait_recv()

    for q in (1, 2):
        send_one[q].wait_recv()
        masked(got_one.at[q - 1], q, 0)

    def solve(p, c, got, total):
        first, second = got[0, :, c], got[1, :, c]
        if p == 0:
            return total + plain(a.at[1], first) + plain(a.at[2], second)
        if p == 1:
            return total + plain(near.at[0], first) + plain(near.at[1], second)
        return total + turned(near.at[1], first) + plain(far, second)

    def negated(p, level, total):
        return -total * kept(p, level) if p else -total

    near_1.wait_recv()

    @pl.when(odd)
    def _():
        far_odd.wait_recv()

    for p in (2, 1, 0):
        @columns(block)
        def _(c):
            total = solve(p, c, got_one, part_one[p, :, c])
            inv_one[p, :, c] = negated(p, 0, total).astype(jnp.bfloat16)

        if p:
            @pl.when(lower | last if p == 2 else lower)
            def _():
                give_one[p].start()

    stores = []

    def store(source, target):
        stores.append(pltpu.make_async_copy(source, target, store_sem.at[len(stores)]))
        stores[-1].start()

    store(inv_one.at[0], out.at[0])

    for p in (2, 1, 0):
        @columns(block)
        def _(c):
            part_two[p, :, c] += plain(inv_one.at[p], par[:, c])

    @columns(block)
    def _(c):
        total = dinv_one[:, c].astype(jnp.float32) - turned(one, inv_one[0, :, c])
        for q in (1, 2):
            total = total - turned(got_one.at[q - 1], inv_one[q, :, c])
        diag_one[:, c] = total.astype(jnp.bfloat16)

    store(diag_one, out.at[6])

    @pl.when(upper)
    def _():
        pl.semaphore_wait(go_sem, 1)

        @pl.when(jnp.logical_not(last))
        def _():
            give_one[2].start()

        @pl.when(odd)
        def _():
            pl.semaphore_signal(go_sem, inc=1, device_id={"row": down[1]}, device_id_type=MESH)

        give_one[1].start()

    def let_go(here):
        @pl.when(here)
        def _():
            pl.semaphore_signal(go_sem, inc=1, device_id={"row": down[2]}, device_id_type=MESH)

    wrap = me == 1
    send_two[1].wait_recv()
    let_go(wrap)
    send_two[2].wait_recv()
    let_go(lower & odd & jnp.logical_not(wrap))
    send_two[0].wait_recv()
    masked(got_two.at[1], 2, 1)
    send_two[3].wait_recv()
    masked(got_two.at[0], 1, 1)
    for p in (1, 2, 0):
        @columns(block)
        def _(c):
            total = solve(p, c, got_two, part_two[p, :, c])
            inv_two[p, :, c] = negated(p, 1, total).astype(jnp.bfloat16)

        if p:
            give_two[p].start()

    store(inv_two.at[0], out.at[3])

    @columns(block)
    def _(c):
        total = plain(diag_one, par[:, c]) + turned(inv_one.at[0], two[:, c])
        for q in (1, 2):
            total = total + turned(inv_one.at[q], got_two[q - 1, :, c])
        cross[:, c] = (-total).astype(jnp.bfloat16)

    store(cross, out.at[7])

    @columns(block)
    def _(c):
        total = dinv_two[:, c].astype(jnp.float32) - turned(par, cross[:, c])
        total = total - turned(two, inv_two[0, :, c])
        for q in (1, 2):
            total = total - turned(got_two.at[q - 1], inv_two[q, :, c])
        diag_two[:, c] = total.astype(jnp.bfloat16)

    store(diag_two, out.at[8])

    @pl.when(odd)
    def _():
        far_pass.wait_send()

    @pl.when(odd)
    def _():
        far_odd.wait_send()

    for copy in [near_0, near_1] + send_two:
        copy.wait_send()
    for group in (send_flags, send_one, give_one, give_two):
        for q in (1, 2):
            group[q].wait_send()
    for item in stores:
        item.wait()
    for give in (give_one, give_two):
        for p in (1, 2):
            give[p].wait_recv()


def place(held, o_inv_one, o_diag_one, o_inv_two, o_cross, o_diag_two, sem):
    copies = [
        pltpu.make_async_copy(source, target, sem.at[i])
        for i, (source, target) in enumerate(
            [
                (held.at[pl.ds(0, 3)], o_inv_one.at[0]),
                (held.at[pl.ds(3, 3)], o_inv_two.at[0]),
                (held.at[6], o_diag_one.at[0]),
                (held.at[7], o_cross.at[0]),
                (held.at[8], o_diag_two.at[0]),
            ]
        )
    ]
    for copy in copies:
        copy.start()
    for copy in copies:
        copy.wait()


def body(anc_band, panel_one, mask_one, dinv_one, panel_two, mask_two, par_two, dinv_two):
    block = anc_band.shape[2]
    kind = anc_band.dtype

    def blocks(number, dtype=kind):
        lead = () if number is None else (number,)
        return pltpu.VMEM(lead + (block, block), dtype)

    hbm = pl.BlockSpec(memory_space=pltpu.HBM)
    free = pl.BlockSpec(memory_space=pl.ANY)
    count = lax.axis_size("row")
    held = pl.pallas_call(
        functools.partial(kernel, count),
        out_shape=pltpu.VMEM((9, block, block), kind),
        in_specs=[hbm] * 8,
        out_specs=free,
        scratch_shapes=[
            blocks(3), blocks(None), blocks(None), blocks(None), blocks(None), blocks(None),
            blocks(2), blocks(None), blocks(2), blocks(2), blocks(3), blocks(3),
            blocks(None), blocks(None), blocks(None), blocks(3, jnp.float32), blocks(3, jnp.float32),
            pltpu.SMEM(mask_one.shape, jnp.int32), pltpu.SMEM(mask_two.shape, jnp.int32),
            pltpu.VMEM((8, 128), jnp.float32), pltpu.VMEM((2, 8, 128), jnp.float32),
            pltpu.SemaphoreType.DMA((8,)),
            pltpu.SemaphoreType.DMA((5,)),
            pltpu.SemaphoreType.DMA((17,)),
            pltpu.SemaphoreType.DMA((16,)),
            pltpu.SemaphoreType.REGULAR,
        ],
        compiler_params=pltpu.CompilerParams(
            collective_id=0, has_side_effects=True, vmem_limit_bytes=40 * 2**20
        ),
    )(*(
        pltpu.with_memory_space_constraint(x, pltpu.HBM)
        for x in (mask_one, mask_two, anc_band, panel_one, dinv_one, panel_two, par_two, dinv_two)
    ))
    return pl.pallas_call(
        place,
        out_shape=[
            jax.ShapeDtypeStruct(anc_band.shape, kind),
            jax.ShapeDtypeStruct(dinv_one.shape, kind),
            jax.ShapeDtypeStruct(anc_band.shape, kind),
            jax.ShapeDtypeStruct(dinv_one.shape, kind),
            jax.ShapeDtypeStruct(dinv_one.shape, kind),
        ],
        in_specs=[free],
        out_specs=[hbm] * 5,
        scratch_shapes=[pltpu.SemaphoreType.DMA((5,))],
        compiler_params=pltpu.CompilerParams(vmem_limit_bytes=2**20),
    )(held)


def solution(mesh):
    four = P(("pole", "row"), None, None, None)
    three = P(("pole", "row"), None, None)
    two = P(("pole", "row"), None)
    return jax.shard_map(
        body,
        mesh=mesh,
        in_specs=(four, four, two, three, four, two, three, three),
        out_specs=(four, three, four, three, three),
        check_vma=False,
    )
```

```python
import functools

import jax
import jax.numpy as jnp
from jax import lax
from jax.experimental import pallas as pl
from jax.experimental.pallas import tpu as pltpu
from jax.sharding import PartitionSpec as P

TILE = 256
DETOUR = 80
MESH = pl.DeviceIdType.MESH


def columns(block):
    def wrap(step):
        @pl.loop(0, block // TILE)
        def _(c):
            step(pl.ds(pl.multiple_of(c * TILE, TILE), TILE))

    return wrap


def plain(left, right):
    return jnp.dot(left[...], right, preferred_element_type=jnp.float32)


def turned(left, right):
    return lax.dot_general(
        left[...], right, (((0,), (0,)), ((), ())), preferred_element_type=jnp.float32
    )


def kernel(
    count,
    mask_one, mask_two, anc, p_one, d_one, p_two, par_in, d_two,
    out,
    a, one, two, par, dinv_one, dinv_two,
    near, far, got_one, got_two, inv_one, inv_two,
    diag_one, cross, diag_two, part_one, part_two, m_one, m_two, flags, got_flags, via,
    load_sem, store_sem, send_sem, recv_sem, go_sem,
):
    block = par.shape[0]
    me = lax.axis_index("row")
    odd = lax.rem(me, 2) == 1
    upper = lax.rem(me, 4) >= 2
    lower = jnp.logical_not(upper)
    last = me >= count - 2
    aside, rest = pl.ds(0, DETOUR), pl.ds(DETOUR, block - DETOUR)
    sends_aside, relays, gets_aside = [(me == count - i) | (me == count - i - 2) for i in (3, 5, 1)]
    bounds = (0, block * 3 // 16, block // 2, block)
    pieces = [pl.ds(a, b - a) for a, b in zip(bounds, bounds[1:])]
    up = [None] + [lax.rem(me + q, count) for q in (1, 2)]
    down = [None] + [lax.rem(me + count - q, count) for q in (1, 2)]

    loads = [
        pltpu.make_async_copy(source, target, load_sem.at[i])
        for i, (source, target) in enumerate(
            [
                (mask_one, m_one),
                (mask_two, m_two),
                (p_one.at[0, 0], one),
                (anc.at[0], a),
                (p_two.at[0, 0], two),
                (par_in.at[0], par),
                (d_one.at[0], dinv_one),
                (d_two.at[0], dinv_two),
            ]
        )
    ]
    barrier = pltpu.get_barrier_semaphore()
    for peer in up[1:]:
        pl.semaphore_signal(barrier, inc=1, device_id={"row": peer}, device_id_type=MESH)
    for load in loads:
        load.start()
    pl.semaphore_wait(barrier, 2)

    def remote(source, target, send, recv, peer):
        return pltpu.make_async_remote_copy(
            src_ref=source,
            dst_ref=target,
            send_sem=send_sem.at[send],
            recv_sem=recv_sem.at[recv],
            device_id={"row": peer},
            device_id_type=MESH,
        )

    near_0 = remote(anc.at[0, 0], near.at[0], 0, 0, down[1])
    near_1 = remote(anc.at[0, 1], near.at[1], 1, 1, down[1])
    far_odd = remote(anc.at[0, 0], far, 2, 2, down[2])
    far_pass = remote(near.at[0], far, 7, 2, down[1])
    send_one = [None] + [remote(p_one.at[0, q], got_one.at[q - 1], 2 + q, 2 + q, down[q]) for q in (1, 2)]
    send_two = [None] + [remote(p_two.at[0, q], got_two.at[q - 1], 4 + q, 4 + q, down[q]) for q in (1, 2)]
    send_two = send_two[2:] + [
        remote(p_two.at[0, 1, piece], got_two.at[0, piece], 14 + i, 13 + i, down[1])
        for i, piece in enumerate(pieces)
    ]
    send_flags = [None] + [remote(flags, got_flags.at[q - 1], 7 + q, 6 + q, down[q]) for q in (1, 2)]
    give_one = [None] + [remote(inv_one.at[p], out.at[p], 9 + p, 8 + p, up[p]) for p in (1, 2)]
    give_part = remote(inv_one.at[2, rest], out.at[2, rest], 11, 10, up[2])
    detour = remote(inv_one.at[2, aside], via, 17, 16, down[2])
    onward = remote(via, out.at[2, aside], 18, 17, lax.rem(me + 4, count))
    give_two = [None] + [remote(inv_two.at[p], out.at[3 + p], 11 + p, 10 + p, up[p]) for p in (1, 2)]

    near_0.start()
    loads[0].wait()
    loads[1].wait()
    flag_one = [None] + [m_one[0, q].astype(jnp.float32) for q in (1, 2)]
    flag_two = [None] + [flag_one[q] * m_two[0, q].astype(jnp.float32) for q in (1, 2)]
    spot = lax.broadcasted_iota(jnp.int32, flags.shape, 0)
    value = jnp.where(spot == 0, flag_one[1], flag_one[2])
    value = jnp.where(spot == 2, flag_two[1], value)
    flags[...] = jnp.where(spot == 3, flag_two[2], value)
    for q in (2, 1):
        send_flags[q].start()
    send_one[2].start()
    send_one[1].start()
    near_1.start()

    @pl.when(odd)
    def _():
        far_odd.start()

    for copy in send_two:
        copy.start()

    def kept(p, level):
        return got_flags[p - 1, pl.ds(2 * level + p - 1, 1), 0:1]

    def masked(ref, q, level):
        flag = kept(q, level).astype(ref.dtype)

        @pl.loop(0, block // 64)
        def _(r):
            rows = pl.ds(pl.multiple_of(r * 64, 64), 64)
            ref[rows, :] = ref[rows, :] * flag

    for load in loads[2:]:
        load.wait()

    @columns(block)
    def _(c):
        for part, own in ((part_one, one), (part_two, two)):
            part[0, :, c] = plain(a.at[0], own[:, c])
            for p in (1, 2):
                part[p, :, c] = turned(a.at[p], own[:, c])

    near_0.wait_recv()

    @pl.when(jnp.logical_not(odd))
    def _():
        far_odd.wait_recv()

    @pl.when(odd)
    def _():
        far_pass.start()

    for q in (1, 2):
        send_flags[q].wait_recv()

    for q in (1, 2):
        send_one[q].wait_recv()
        masked(got_one.at[q - 1], q, 0)

    def solve(p, c, got, total):
        first, second = got[0, :, c], got[1, :, c]
        if p == 0:
            return total + plain(a.at[1], first) + plain(a.at[2], second)
        if p == 1:
            return total + plain(near.at[0], first) + plain(near.at[1], second)
        return total + turned(near.at[1], first) + plain(far, second)

    def give_far():
        @pl.when(sends_aside)
        def _():
            give_part.start()

        @pl.when(jnp.logical_not(sends_aside))
        def _():
            give_one[2].start()

    def negated(p, level, total):
        return -total * kept(p, level) if p else -total

    near_1.wait_recv()

    @pl.when(odd)
    def _():
        far_odd.wait_recv()

    for p in (2, 1, 0):
        @columns(block)
        def _(c):
            total = solve(p, c, got_one, part_one[p, :, c])
            inv_one[p, :, c] = negated(p, 0, total).astype(jnp.bfloat16)

        if p == 2:
            @pl.when(sends_aside)
            def _():
                detour.start()

            @pl.when(lower | last)
            def _():
                give_far()

        if p == 1:
            @pl.when(lower)
            def _():
                give_one[1].start()

    stores = []

    def store(source, target):
        stores.append(pltpu.make_async_copy(source, target, store_sem.at[len(stores)]))
        stores[-1].start()

    store(inv_one.at[0], out.at[0])

    for p in (2, 1, 0):
        @columns(block)
        def _(c):
            part_two[p, :, c] += plain(inv_one.at[p], par[:, c])

    @columns(block)
    def _(c):
        total = dinv_one[:, c].astype(jnp.float32) - turned(one, inv_one[0, :, c])
        for q in (1, 2):
            total = total - turned(got_one.at[q - 1], inv_one[q, :, c])
        diag_one[:, c] = total.astype(jnp.bfloat16)

    store(diag_one, out.at[6])

    @pl.when(upper)
    def _():
        pl.semaphore_wait(go_sem, 1)

        @pl.when(jnp.logical_not(last))
        def _():
            give_far()

        @pl.when(odd)
        def _():
            pl.semaphore_signal(go_sem, inc=1, device_id={"row": down[1]}, device_id_type=MESH)

        give_one[1].start()

    def let_go(here):
        @pl.when(here)
        def _():
            pl.semaphore_signal(go_sem, inc=1, device_id={"row": down[2]}, device_id_type=MESH)

    wrap = me == 1
    send_two[1].wait_recv()
    let_go(wrap)
    send_two[2].wait_recv()
    let_go(lower & odd & jnp.logical_not(wrap))
    send_two[0].wait_recv()
    masked(got_two.at[1], 2, 1)
    send_two[3].wait_recv()
    masked(got_two.at[0], 1, 1)
    for p in (1, 2, 0):
        @columns(block)
        def _(c):
            total = solve(p, c, got_two, part_two[p, :, c])
            inv_two[p, :, c] = negated(p, 1, total).astype(jnp.bfloat16)

        if p:
            give_two[p].start()

    store(inv_two.at[0], out.at[3])

    @pl.when(relays)
    def _():
        detour.wait_recv()
        onward.start()

    @columns(block)
    def _(c):
        total = plain(diag_one, par[:, c]) + turned(inv_one.at[0], two[:, c])
        for q in (1, 2):
            total = total + turned(inv_one.at[q], got_two[q - 1, :, c])
        cross[:, c] = (-total).astype(jnp.bfloat16)

    store(cross, out.at[7])

    @columns(block)
    def _(c):
        total = dinv_two[:, c].astype(jnp.float32) - turned(par, cross[:, c])
        total = total - turned(two, inv_two[0, :, c])
        for q in (1, 2):
            total = total - turned(got_two.at[q - 1], inv_two[q, :, c])
        diag_two[:, c] = total.astype(jnp.bfloat16)

    store(diag_two, out.at[8])

    @pl.when(odd)
    def _():
        far_pass.wait_send()

    @pl.when(odd)
    def _():
        far_odd.wait_send()

    for copy in [near_0, near_1] + send_two:
        copy.wait_send()
    for group in (send_flags, send_one, give_two):
        for q in (1, 2):
            group[q].wait_send()
    give_one[1].wait_send()

    @pl.when(sends_aside)
    def _():
        give_part.wait_send()
        detour.wait_send()

    @pl.when(jnp.logical_not(sends_aside))
    def _():
        give_one[2].wait_send()

    for item in stores:
        item.wait()

    @pl.when(gets_aside)
    def _():
        give_part.wait_recv()
        onward.wait_recv()

    @pl.when(jnp.logical_not(gets_aside))
    def _():
        give_one[2].wait_recv()

    @pl.when(relays)
    def _():
        onward.wait_send()

    for give in (give_one[1], give_two[1], give_two[2]):
        give.wait_recv()


def place(held, o_inv_one, o_diag_one, o_inv_two, o_cross, o_diag_two, sem):
    copies = [
        pltpu.make_async_copy(source, target, sem.at[i])
        for i, (source, target) in enumerate(
            [
                (held.at[pl.ds(0, 3)], o_inv_one.at[0]),
                (held.at[pl.ds(3, 3)], o_inv_two.at[0]),
                (held.at[6], o_diag_one.at[0]),
                (held.at[7], o_cross.at[0]),
                (held.at[8], o_diag_two.at[0]),
            ]
        )
    ]
    for copy in copies:
        copy.start()
    for copy in copies:
        copy.wait()


def body(anc_band, panel_one, mask_one, dinv_one, panel_two, mask_two, par_two, dinv_two):
    block = anc_band.shape[2]
    kind = anc_band.dtype

    def blocks(number, dtype=kind):
        lead = () if number is None else (number,)
        return pltpu.VMEM(lead + (block, block), dtype)

    hbm = pl.BlockSpec(memory_space=pltpu.HBM)
    free = pl.BlockSpec(memory_space=pl.ANY)
    count = lax.axis_size("row")
    held = pl.pallas_call(
        functools.partial(kernel, count),
        out_shape=pltpu.VMEM((9, block, block), kind),
        in_specs=[hbm] * 8,
        out_specs=free,
        scratch_shapes=[
            blocks(3), blocks(None), blocks(None), blocks(None), blocks(None), blocks(None),
            blocks(2), blocks(None), blocks(2), blocks(2), blocks(3), blocks(3),
            blocks(None), blocks(None), blocks(None), blocks(3, jnp.float32), blocks(3, jnp.float32),
            pltpu.SMEM(mask_one.shape, jnp.int32), pltpu.SMEM(mask_two.shape, jnp.int32),
            pltpu.VMEM((8, 128), jnp.float32), pltpu.VMEM((2, 8, 128), jnp.float32), pltpu.VMEM((DETOUR, block), kind),
            pltpu.SemaphoreType.DMA((8,)),
            pltpu.SemaphoreType.DMA((5,)),
            pltpu.SemaphoreType.DMA((19,)),
            pltpu.SemaphoreType.DMA((18,)),
            pltpu.SemaphoreType.REGULAR,
        ],
        compiler_params=pltpu.CompilerParams(
            collective_id=0, has_side_effects=True, vmem_limit_bytes=40 * 2**20
        ),
    )(*(
        pltpu.with_memory_space_constraint(x, pltpu.HBM)
        for x in (mask_one, mask_two, anc_band, panel_one, dinv_one, panel_two, par_two, dinv_two)
    ))
    return pl.pallas_call(
        place,
        out_shape=[
            jax.ShapeDtypeStruct(anc_band.shape, kind),
            jax.ShapeDtypeStruct(dinv_one.shape, kind),
            jax.ShapeDtypeStruct(anc_band.shape, kind),
            jax.ShapeDtypeStruct(dinv_one.shape, kind),
            jax.ShapeDtypeStruct(dinv_one.shape, kind),
        ],
        in_specs=[free],
        out_specs=[hbm] * 5,
        scratch_shapes=[pltpu.SemaphoreType.DMA((5,))],
        compiler_params=pltpu.CompilerParams(vmem_limit_bytes=2**20),
    )(held)


def solution(mesh):
    four = P(("pole", "row"), None, None, None)
    three = P(("pole", "row"), None, None)
    two = P(("pole", "row"), None)
    return jax.shard_map(
        body,
        mesh=mesh,
        in_specs=(four, four, two, three, four, two, three, three),
        out_specs=(four, three, four, three, three),
        check_vma=False,
    )
```

```python
import functools

import jax
import jax.numpy as jnp
from jax import lax
from jax.experimental import pallas as pl
from jax.experimental.pallas import tpu as pltpu
from jax.sharding import PartitionSpec as P

TILE = 256
DETOURS = {3: 112, 7: 80, 11: 48, 5: 80, 9: 48}
MESH = pl.DeviceIdType.MESH


def columns(block):
    def wrap(step):
        @pl.loop(0, block // TILE)
        def _(c):
            step(pl.ds(pl.multiple_of(c * TILE, TILE), TILE))

    return wrap


def plain(left, right):
    return jnp.dot(left[...], right, preferred_element_type=jnp.float32)


def turned(left, right):
    return lax.dot_general(
        left[...], right, (((0,), (0,)), ((), ())), preferred_element_type=jnp.float32
    )


def kernel(
    count,
    mask_one, mask_two, anc, p_one, d_one, p_two, par_in, d_two,
    out,
    a, one, two, par, dinv_one, dinv_two,
    near, far, got_one, got_two, inv_one, inv_two,
    diag_one, cross, diag_two, part_one, part_two, m_one, m_two, flags, got_flags, via,
    load_sem, store_sem, send_sem, recv_sem, go_sem,
):
    block = par.shape[0]
    me = lax.axis_index("row")
    odd = lax.rem(me, 2) == 1
    upper = lax.rem(me, 4) >= 2
    lower = jnp.logical_not(upper)
    last = me >= count - 2
    def at(places):
        return functools.reduce(jnp.logical_or, [me == count - i for i in places])

    asides = {
        size: [i for i in DETOURS if DETOURS[i] == size] for size in sorted(set(DETOURS.values()))
    }
    sends_aside = at(DETOURS)
    bounds = (0, block * 3 // 16, block // 2, block)
    pieces = [pl.ds(a, b - a) for a, b in zip(bounds, bounds[1:])]
    up = [None] + [lax.rem(me + q, count) for q in (1, 2)]
    down = [None] + [lax.rem(me + count - q, count) for q in (1, 2)]

    loads = [
        pltpu.make_async_copy(source, target, load_sem.at[i])
        for i, (source, target) in enumerate(
            [
                (mask_one, m_one),
                (mask_two, m_two),
                (p_one.at[0, 0], one),
                (anc.at[0], a),
                (p_two.at[0, 0], two),
                (par_in.at[0], par),
                (d_one.at[0], dinv_one),
                (d_two.at[0], dinv_two),
            ]
        )
    ]
    barrier = pltpu.get_barrier_semaphore()
    for peer in up[1:]:
        pl.semaphore_signal(barrier, inc=1, device_id={"row": peer}, device_id_type=MESH)
    for load in loads:
        load.start()
    pl.semaphore_wait(barrier, 2)

    def remote(source, target, send, recv, peer):
        return pltpu.make_async_remote_copy(
            src_ref=source,
            dst_ref=target,
            send_sem=send_sem.at[send],
            recv_sem=recv_sem.at[recv],
            device_id={"row": peer},
            device_id_type=MESH,
        )

    near_0 = remote(anc.at[0, 0], near.at[0], 0, 0, down[1])
    near_1 = remote(anc.at[0, 1], near.at[1], 1, 1, down[1])
    far_odd = remote(anc.at[0, 0], far, 2, 2, down[2])
    far_pass = remote(near.at[0], far, 7, 2, down[1])
    send_one = [None] + [remote(p_one.at[0, q], got_one.at[q - 1], 2 + q, 2 + q, down[q]) for q in (1, 2)]
    send_two = [None] + [remote(p_two.at[0, q], got_two.at[q - 1], 4 + q, 4 + q, down[q]) for q in (1, 2)]
    send_two = send_two[2:] + [
        remote(p_two.at[0, 1, piece], got_two.at[0, piece], 14 + i, 13 + i, down[1])
        for i, piece in enumerate(pieces)
    ]
    send_flags = [None] + [remote(flags, got_flags.at[q - 1], 7 + q, 6 + q, down[q]) for q in (1, 2)]
    give_one = [None] + [remote(inv_one.at[p], out.at[p], 9 + p, 8 + p, up[p]) for p in (1, 2)]
    def part(size):
        rest = pl.ds(size, block - size)
        return remote(inv_one.at[2, rest], out.at[2, rest], 11, 10, up[2])

    def detour(size):
        aside = pl.ds(0, size)
        return remote(inv_one.at[2, aside], via.at[aside], 17, 16, down[2])

    def onward(size):
        aside = pl.ds(0, size)
        return remote(via.at[aside], out.at[2, aside], 18, 17, lax.rem(me + 4, count))

    def by_size(shift, act):
        for size, places in asides.items():
            @pl.when(at([i + shift for i in places]))
            def _():
                act(size)

    give_two = [None] + [remote(inv_two.at[p], out.at[3 + p], 11 + p, 10 + p, up[p]) for p in (1, 2)]

    near_0.start()
    loads[0].wait()
    loads[1].wait()
    flag_one = [None] + [m_one[0, q].astype(jnp.float32) for q in (1, 2)]
    flag_two = [None] + [flag_one[q] * m_two[0, q].astype(jnp.float32) for q in (1, 2)]
    spot = lax.broadcasted_iota(jnp.int32, flags.shape, 0)
    value = jnp.where(spot == 0, flag_one[1], flag_one[2])
    value = jnp.where(spot == 2, flag_two[1], value)
    flags[...] = jnp.where(spot == 3, flag_two[2], value)
    for q in (2, 1):
        send_flags[q].start()
    send_one[2].start()
    send_one[1].start()
    near_1.start()

    @pl.when(odd)
    def _():
        far_odd.start()

    for copy in send_two:
        copy.start()

    def kept(p, level):
        return got_flags[p - 1, pl.ds(2 * level + p - 1, 1), 0:1]

    def masked(ref, q, level):
        flag = kept(q, level).astype(ref.dtype)

        @pl.loop(0, block // 64)
        def _(r):
            rows = pl.ds(pl.multiple_of(r * 64, 64), 64)
            ref[rows, :] = ref[rows, :] * flag

    for load in loads[2:]:
        load.wait()

    @columns(block)
    def _(c):
        for part, own in ((part_one, one), (part_two, two)):
            part[0, :, c] = plain(a.at[0], own[:, c])
            for p in (1, 2):
                part[p, :, c] = turned(a.at[p], own[:, c])

    near_0.wait_recv()

    @pl.when(jnp.logical_not(odd))
    def _():
        far_odd.wait_recv()

    @pl.when(odd)
    def _():
        far_pass.start()

    for q in (1, 2):
        send_flags[q].wait_recv()

    for q in (1, 2):
        send_one[q].wait_recv()
        masked(got_one.at[q - 1], q, 0)

    def solve(p, c, got, total):
        first, second = got[0, :, c], got[1, :, c]
        if p == 0:
            return total + plain(a.at[1], first) + plain(a.at[2], second)
        if p == 1:
            return total + plain(near.at[0], first) + plain(near.at[1], second)
        return total + turned(near.at[1], first) + plain(far, second)

    def give_far():
        by_size(0, lambda size: part(size).start())

        @pl.when(jnp.logical_not(sends_aside))
        def _():
            give_one[2].start()

    def negated(p, level, total):
        return -total * kept(p, level) if p else -total

    near_1.wait_recv()

    @pl.when(odd)
    def _():
        far_odd.wait_recv()

    for p in (2, 1, 0):
        @columns(block)
        def _(c):
            total = solve(p, c, got_one, part_one[p, :, c])
            inv_one[p, :, c] = negated(p, 0, total).astype(jnp.bfloat16)

        if p == 2:
            by_size(0, lambda size: detour(size).start())

            @pl.when(lower | last)
            def _():
                give_far()

        if p == 1:
            @pl.when(lower)
            def _():
                give_one[1].start()

    stores = []

    def store(source, target):
        stores.append(pltpu.make_async_copy(source, target, store_sem.at[len(stores)]))
        stores[-1].start()

    store(inv_one.at[0], out.at[0])

    for p in (2, 1, 0):
        @columns(block)
        def _(c):
            part_two[p, :, c] += plain(inv_one.at[p], par[:, c])

    @columns(block)
    def _(c):
        total = dinv_one[:, c].astype(jnp.float32) - turned(one, inv_one[0, :, c])
        for q in (1, 2):
            total = total - turned(got_one.at[q - 1], inv_one[q, :, c])
        diag_one[:, c] = total.astype(jnp.bfloat16)

    store(diag_one, out.at[6])

    @pl.when(upper)
    def _():
        pl.semaphore_wait(go_sem, 1)

        @pl.when(jnp.logical_not(last))
        def _():
            give_far()

        @pl.when(odd)
        def _():
            pl.semaphore_signal(go_sem, inc=1, device_id={"row": down[1]}, device_id_type=MESH)

        give_one[1].start()

    def let_go(here):
        @pl.when(here)
        def _():
            pl.semaphore_signal(go_sem, inc=1, device_id={"row": down[2]}, device_id_type=MESH)

    wrap = me == 1
    send_two[1].wait_recv()
    let_go(wrap)
    send_two[2].wait_recv()
    let_go(lower & odd & jnp.logical_not(wrap))
    send_two[0].wait_recv()
    masked(got_two.at[1], 2, 1)
    send_two[3].wait_recv()
    masked(got_two.at[0], 1, 1)
    for p in (1, 2, 0):
        @columns(block)
        def _(c):
            total = solve(p, c, got_two, part_two[p, :, c])
            inv_two[p, :, c] = negated(p, 1, total).astype(jnp.bfloat16)

        if p:
            give_two[p].start()

    store(inv_two.at[0], out.at[3])

    def pass_on(size):
        detour(size).wait_recv()
        onward(size).start()

    by_size(2, pass_on)

    @columns(block)
    def _(c):
        total = plain(diag_one, par[:, c]) + turned(inv_one.at[0], two[:, c])
        for q in (1, 2):
            total = total + turned(inv_one.at[q], got_two[q - 1, :, c])
        cross[:, c] = (-total).astype(jnp.bfloat16)

    store(cross, out.at[7])

    @columns(block)
    def _(c):
        total = dinv_two[:, c].astype(jnp.float32) - turned(par, cross[:, c])
        total = total - turned(two, inv_two[0, :, c])
        for q in (1, 2):
            total = total - turned(got_two.at[q - 1], inv_two[q, :, c])
        diag_two[:, c] = total.astype(jnp.bfloat16)

    store(diag_two, out.at[8])

    @pl.when(odd)
    def _():
        far_pass.wait_send()

    @pl.when(odd)
    def _():
        far_odd.wait_send()

    for copy in [near_0, near_1] + send_two:
        copy.wait_send()
    for group in (send_flags, send_one, give_two):
        for q in (1, 2):
            group[q].wait_send()
    give_one[1].wait_send()

    def aside_sent(size):
        part(size).wait_send()
        detour(size).wait_send()

    by_size(0, aside_sent)

    @pl.when(jnp.logical_not(sends_aside))
    def _():
        give_one[2].wait_send()

    for item in stores:
        item.wait()

    def aside_here(size):
        part(size).wait_recv()
        onward(size).wait_recv()

    by_size(-2, aside_here)

    @pl.when(jnp.logical_not(at([i - 2 for i in DETOURS])))
    def _():
        give_one[2].wait_recv()

    by_size(2, lambda size: onward(size).wait_send())

    for give in (give_one[1], give_two[1], give_two[2]):
        give.wait_recv()


def place(held, o_inv_one, o_diag_one, o_inv_two, o_cross, o_diag_two, sem):
    copies = [
        pltpu.make_async_copy(source, target, sem.at[i])
        for i, (source, target) in enumerate(
            [
                (held.at[pl.ds(0, 3)], o_inv_one.at[0]),
                (held.at[pl.ds(3, 3)], o_inv_two.at[0]),
                (held.at[6], o_diag_one.at[0]),
                (held.at[7], o_cross.at[0]),
                (held.at[8], o_diag_two.at[0]),
            ]
        )
    ]
    for copy in copies:
        copy.start()
    for copy in copies:
        copy.wait()


def body(anc_band, panel_one, mask_one, dinv_one, panel_two, mask_two, par_two, dinv_two):
    block = anc_band.shape[2]
    kind = anc_band.dtype

    def blocks(number, dtype=kind):
        lead = () if number is None else (number,)
        return pltpu.VMEM(lead + (block, block), dtype)

    hbm = pl.BlockSpec(memory_space=pltpu.HBM)
    free = pl.BlockSpec(memory_space=pl.ANY)
    count = lax.axis_size("row")
    held = pl.pallas_call(
        functools.partial(kernel, count),
        out_shape=pltpu.VMEM((9, block, block), kind),
        in_specs=[hbm] * 8,
        out_specs=free,
        scratch_shapes=[
            blocks(3), blocks(None), blocks(None), blocks(None), blocks(None), blocks(None),
            blocks(2), blocks(None), blocks(2), blocks(2), blocks(3), blocks(3),
            blocks(None), blocks(None), blocks(None), blocks(3, jnp.float32), blocks(3, jnp.float32),
            pltpu.SMEM(mask_one.shape, jnp.int32), pltpu.SMEM(mask_two.shape, jnp.int32),
            pltpu.VMEM((8, 128), jnp.float32), pltpu.VMEM((2, 8, 128), jnp.float32), pltpu.VMEM((max(DETOURS.values()), block), kind),
            pltpu.SemaphoreType.DMA((8,)),
            pltpu.SemaphoreType.DMA((5,)),
            pltpu.SemaphoreType.DMA((19,)),
            pltpu.SemaphoreType.DMA((18,)),
            pltpu.SemaphoreType.REGULAR,
        ],
        compiler_params=pltpu.CompilerParams(
            collective_id=0, has_side_effects=True, vmem_limit_bytes=40 * 2**20
        ),
    )(*(
        pltpu.with_memory_space_constraint(x, pltpu.HBM)
        for x in (mask_one, mask_two, anc_band, panel_one, dinv_one, panel_two, par_two, dinv_two)
    ))
    return pl.pallas_call(
        place,
        out_shape=[
            jax.ShapeDtypeStruct(anc_band.shape, kind),
            jax.ShapeDtypeStruct(dinv_one.shape, kind),
            jax.ShapeDtypeStruct(anc_band.shape, kind),
            jax.ShapeDtypeStruct(dinv_one.shape, kind),
            jax.ShapeDtypeStruct(dinv_one.shape, kind),
        ],
        in_specs=[free],
        out_specs=[hbm] * 5,
        scratch_shapes=[pltpu.SemaphoreType.DMA((5,))],
        compiler_params=pltpu.CompilerParams(vmem_limit_bytes=2**20),
    )(held)


def solution(mesh):
    four = P(("pole", "row"), None, None, None)
    three = P(("pole", "row"), None, None)
    two = P(("pole", "row"), None)
    return jax.shard_map(
        body,
        mesh=mesh,
        in_specs=(four, four, two, three, four, two, three, three),
        out_specs=(four, three, four, three, three),
        check_vma=False,
    )
```

```python
import functools

import jax
import jax.numpy as jnp
from jax import lax
from jax.experimental import pallas as pl
from jax.experimental.pallas import tpu as pltpu
from jax.sharding import PartitionSpec as P

TILE = 256
DETOURS = {3: 112, 7: 80, 11: 32, 5: 48, 9: 16}
MESH = pl.DeviceIdType.MESH


def columns(block):
    def wrap(step):
        @pl.loop(0, block // TILE)
        def _(c):
            step(pl.ds(pl.multiple_of(c * TILE, TILE), TILE))

    return wrap


def plain(left, right):
    return jnp.dot(left[...], right, preferred_element_type=jnp.float32)


def turned(left, right):
    return lax.dot_general(
        left[...], right, (((0,), (0,)), ((), ())), preferred_element_type=jnp.float32
    )


def kernel(
    count,
    mask_one, mask_two, anc, p_one, d_one, p_two, par_in, d_two,
    out,
    a, one, two, par, dinv_one, dinv_two,
    near, far, got_one, got_two, inv_one, inv_two,
    diag_one, cross, diag_two, part_one, part_two, m_one, m_two, flags, got_flags, via,
    load_sem, store_sem, send_sem, recv_sem, go_sem,
):
    block = par.shape[0]
    me = lax.axis_index("row")
    odd = lax.rem(me, 2) == 1
    upper = lax.rem(me, 4) >= 2
    lower = jnp.logical_not(upper)
    last = me >= count - 2
    def at(places):
        return functools.reduce(jnp.logical_or, [me == count - i for i in places])

    asides = {
        size: [i for i in DETOURS if DETOURS[i] == size] for size in sorted(set(DETOURS.values()))
    }
    sends_aside = at(DETOURS)
    bounds = (0, block * 3 // 16, block // 2, block)
    pieces = [pl.ds(a, b - a) for a, b in zip(bounds, bounds[1:])]
    up = [None] + [lax.rem(me + q, count) for q in (1, 2)]
    down = [None] + [lax.rem(me + count - q, count) for q in (1, 2)]

    loads = [
        pltpu.make_async_copy(source, target, load_sem.at[i])
        for i, (source, target) in enumerate(
            [
                (mask_one, m_one),
                (mask_two, m_two),
                (p_one.at[0, 0], one),
                (anc.at[0], a),
                (p_two.at[0, 0], two),
                (par_in.at[0], par),
                (d_one.at[0], dinv_one),
                (d_two.at[0], dinv_two),
            ]
        )
    ]
    barrier = pltpu.get_barrier_semaphore()
    for peer in up[1:]:
        pl.semaphore_signal(barrier, inc=1, device_id={"row": peer}, device_id_type=MESH)
    for load in loads:
        load.start()
    pl.semaphore_wait(barrier, 2)

    def remote(source, target, send, recv, peer):
        return pltpu.make_async_remote_copy(
            src_ref=source,
            dst_ref=target,
            send_sem=send_sem.at[send],
            recv_sem=recv_sem.at[recv],
            device_id={"row": peer},
            device_id_type=MESH,
        )

    near_0 = remote(anc.at[0, 0], near.at[0], 0, 0, down[1])
    near_1 = remote(anc.at[0, 1], near.at[1], 1, 1, down[1])
    far_odd = remote(anc.at[0, 0], far, 2, 2, down[2])
    far_pass = remote(near.at[0], far, 7, 2, down[1])
    send_one = [None] + [remote(p_one.at[0, q], got_one.at[q - 1], 2 + q, 2 + q, down[q]) for q in (1, 2)]
    send_two = [None] + [remote(p_two.at[0, q], got_two.at[q - 1], 4 + q, 4 + q, down[q]) for q in (1, 2)]
    send_two = send_two[2:] + [
        remote(p_two.at[0, 1, piece], got_two.at[0, piece], 14 + i, 13 + i, down[1])
        for i, piece in enumerate(pieces)
    ]
    send_flags = [None] + [remote(flags, got_flags.at[q - 1], 7 + q, 6 + q, down[q]) for q in (1, 2)]
    give_one = [None] + [remote(inv_one.at[p], out.at[p], 9 + p, 8 + p, up[p]) for p in (1, 2)]
    def part(size):
        rest = pl.ds(size, block - size)
        return remote(inv_one.at[2, rest], out.at[2, rest], 11, 10, up[2])

    def detour(size):
        aside = pl.ds(0, size)
        return remote(inv_one.at[2, aside], via.at[aside], 17, 16, down[2])

    def onward(size):
        aside = pl.ds(0, size)
        return remote(via.at[aside], out.at[2, aside], 18, 17, lax.rem(me + 4, count))

    def by_size(shift, act):
        for size, places in asides.items():
            @pl.when(at([i + shift for i in places]))
            def _():
                act(size)

    give_two = [None] + [remote(inv_two.at[p], out.at[3 + p], 11 + p, 10 + p, up[p]) for p in (1, 2)]

    near_0.start()
    loads[0].wait()
    loads[1].wait()
    flag_one = [None] + [m_one[0, q].astype(jnp.float32) for q in (1, 2)]
    flag_two = [None] + [flag_one[q] * m_two[0, q].astype(jnp.float32) for q in (1, 2)]
    spot = lax.broadcasted_iota(jnp.int32, flags.shape, 0)
    value = jnp.where(spot == 0, flag_one[1], flag_one[2])
    value = jnp.where(spot == 2, flag_two[1], value)
    flags[...] = jnp.where(spot == 3, flag_two[2], value)
    for q in (2, 1):
        send_flags[q].start()
    send_one[2].start()
    send_one[1].start()
    near_1.start()

    @pl.when(odd)
    def _():
        far_odd.start()

    for copy in send_two:
        copy.start()

    def kept(p, level):
        return got_flags[p - 1, pl.ds(2 * level + p - 1, 1), 0:1]

    def masked(ref, q, level):
        flag = kept(q, level).astype(ref.dtype)

        @pl.loop(0, block // 64)
        def _(r):
            rows = pl.ds(pl.multiple_of(r * 64, 64), 64)
            ref[rows, :] = ref[rows, :] * flag

    for load in loads[2:]:
        load.wait()

    @columns(block)
    def _(c):
        for part, own in ((part_one, one), (part_two, two)):
            part[0, :, c] = plain(a.at[0], own[:, c])
            for p in (1, 2):
                part[p, :, c] = turned(a.at[p], own[:, c])

    near_0.wait_recv()

    @pl.when(jnp.logical_not(odd))
    def _():
        far_odd.wait_recv()

    @pl.when(odd)
    def _():
        far_pass.start()

    for q in (1, 2):
        send_flags[q].wait_recv()

    for q in (1, 2):
        send_one[q].wait_recv()
        masked(got_one.at[q - 1], q, 0)

    def solve(p, c, got, total):
        first, second = got[0, :, c], got[1, :, c]
        if p == 0:
            return total + plain(a.at[1], first) + plain(a.at[2], second)
        if p == 1:
            return total + plain(near.at[0], first) + plain(near.at[1], second)
        return total + turned(near.at[1], first) + plain(far, second)

    def give_far():
        by_size(0, lambda size: part(size).start())

        @pl.when(jnp.logical_not(sends_aside))
        def _():
            give_one[2].start()

    def negated(p, level, total):
        return -total * kept(p, level) if p else -total

    near_1.wait_recv()

    @pl.when(odd)
    def _():
        far_odd.wait_recv()

    for p in (2, 1, 0):
        @columns(block)
        def _(c):
            total = solve(p, c, got_one, part_one[p, :, c])
            inv_one[p, :, c] = negated(p, 0, total).astype(jnp.bfloat16)

        if p == 2:
            by_size(0, lambda size: detour(size).start())

            @pl.when(lower | last)
            def _():
                give_far()

        if p == 1:
            @pl.when(lower)
            def _():
                give_one[1].start()

    stores = []

    def store(source, target):
        stores.append(pltpu.make_async_copy(source, target, store_sem.at[len(stores)]))
        stores[-1].start()

    store(inv_one.at[0], out.at[0])

    for p in (2, 1, 0):
        @columns(block)
        def _(c):
            part_two[p, :, c] += plain(inv_one.at[p], par[:, c])

    @columns(block)
    def _(c):
        total = dinv_one[:, c].astype(jnp.float32) - turned(one, inv_one[0, :, c])
        for q in (1, 2):
            total = total - turned(got_one.at[q - 1], inv_one[q, :, c])
        diag_one[:, c] = total.astype(jnp.bfloat16)

    store(diag_one, out.at[6])

    @pl.when(upper)
    def _():
        pl.semaphore_wait(go_sem, 1)

        @pl.when(jnp.logical_not(last))
        def _():
            give_far()

        @pl.when(odd)
        def _():
            pl.semaphore_signal(go_sem, inc=1, device_id={"row": down[1]}, device_id_type=MESH)

        give_one[1].start()

    def let_go(here):
        @pl.when(here)
        def _():
            pl.semaphore_signal(go_sem, inc=1, device_id={"row": down[2]}, device_id_type=MESH)

    wrap = me == 1
    send_two[1].wait_recv()
    let_go(wrap)
    send_two[2].wait_recv()
    let_go(lower & odd & jnp.logical_not(wrap))
    send_two[0].wait_recv()
    masked(got_two.at[1], 2, 1)
    send_two[3].wait_recv()
    masked(got_two.at[0], 1, 1)
    for p in (1, 2, 0):
        @columns(block)
        def _(c):
            total = solve(p, c, got_two, part_two[p, :, c])
            inv_two[p, :, c] = negated(p, 1, total).astype(jnp.bfloat16)

        if p:
            give_two[p].start()

    store(inv_two.at[0], out.at[3])

    def pass_on(size):
        detour(size).wait_recv()
        onward(size).start()

    by_size(2, pass_on)

    @columns(block)
    def _(c):
        total = plain(diag_one, par[:, c]) + turned(inv_one.at[0], two[:, c])
        for q in (1, 2):
            total = total + turned(inv_one.at[q], got_two[q - 1, :, c])
        cross[:, c] = (-total).astype(jnp.bfloat16)

    store(cross, out.at[7])

    @columns(block)
    def _(c):
        total = dinv_two[:, c].astype(jnp.float32) - turned(par, cross[:, c])
        total = total - turned(two, inv_two[0, :, c])
        for q in (1, 2):
            total = total - turned(got_two.at[q - 1], inv_two[q, :, c])
        diag_two[:, c] = total.astype(jnp.bfloat16)

    store(diag_two, out.at[8])

    @pl.when(odd)
    def _():
        far_pass.wait_send()

    @pl.when(odd)
    def _():
        far_odd.wait_send()

    for copy in [near_0, near_1] + send_two:
        copy.wait_send()
    for group in (send_flags, send_one, give_two):
        for q in (1, 2):
            group[q].wait_send()
    give_one[1].wait_send()

    def aside_sent(size):
        part(size).wait_send()
        detour(size).wait_send()

    by_size(0, aside_sent)

    @pl.when(jnp.logical_not(sends_aside))
    def _():
        give_one[2].wait_send()

    for item in stores:
        item.wait()

    def aside_here(size):
        part(size).wait_recv()
        onward(size).wait_recv()

    by_size(-2, aside_here)

    @pl.when(jnp.logical_not(at([i - 2 for i in DETOURS])))
    def _():
        give_one[2].wait_recv()

    by_size(2, lambda size: onward(size).wait_send())

    for give in (give_one[1], give_two[1], give_two[2]):
        give.wait_recv()


def place(held, o_inv_one, o_diag_one, o_inv_two, o_cross, o_diag_two, sem):
    copies = [
        pltpu.make_async_copy(source, target, sem.at[i])
        for i, (source, target) in enumerate(
            [
                (held.at[pl.ds(0, 3)], o_inv_one.at[0]),
                (held.at[pl.ds(3, 3)], o_inv_two.at[0]),
                (held.at[6], o_diag_one.at[0]),
                (held.at[7], o_cross.at[0]),
                (held.at[8], o_diag_two.at[0]),
            ]
        )
    ]
    for copy in copies:
        copy.start()
    for copy in copies:
        copy.wait()


def body(anc_band, panel_one, mask_one, dinv_one, panel_two, mask_two, par_two, dinv_two):
    block = anc_band.shape[2]
    kind = anc_band.dtype

    def blocks(number, dtype=kind):
        lead = () if number is None else (number,)
        return pltpu.VMEM(lead + (block, block), dtype)

    hbm = pl.BlockSpec(memory_space=pltpu.HBM)
    free = pl.BlockSpec(memory_space=pl.ANY)
    count = lax.axis_size("row")
    held = pl.pallas_call(
        functools.partial(kernel, count),
        out_shape=pltpu.VMEM((9, block, block), kind),
        in_specs=[hbm] * 8,
        out_specs=free,
        scratch_shapes=[
            blocks(3), blocks(None), blocks(None), blocks(None), blocks(None), blocks(None),
            blocks(2), blocks(None), blocks(2), blocks(2), blocks(3), blocks(3),
            blocks(None), blocks(None), blocks(None), blocks(3, jnp.float32), blocks(3, jnp.float32),
            pltpu.SMEM(mask_one.shape, jnp.int32), pltpu.SMEM(mask_two.shape, jnp.int32),
            pltpu.VMEM((8, 128), jnp.float32), pltpu.VMEM((2, 8, 128), jnp.float32), pltpu.VMEM((max(DETOURS.values()), block), kind),
            pltpu.SemaphoreType.DMA((8,)),
            pltpu.SemaphoreType.DMA((5,)),
            pltpu.SemaphoreType.DMA((19,)),
            pltpu.SemaphoreType.DMA((18,)),
            pltpu.SemaphoreType.REGULAR,
        ],
        compiler_params=pltpu.CompilerParams(
            collective_id=0, has_side_effects=True, vmem_limit_bytes=40 * 2**20
        ),
    )(*(
        pltpu.with_memory_space_constraint(x, pltpu.HBM)
        for x in (mask_one, mask_two, anc_band, panel_one, dinv_one, panel_two, par_two, dinv_two)
    ))
    return pl.pallas_call(
        place,
        out_shape=[
            jax.ShapeDtypeStruct(anc_band.shape, kind),
            jax.ShapeDtypeStruct(dinv_one.shape, kind),
            jax.ShapeDtypeStruct(anc_band.shape, kind),
            jax.ShapeDtypeStruct(dinv_one.shape, kind),
            jax.ShapeDtypeStruct(dinv_one.shape, kind),
        ],
        in_specs=[free],
        out_specs=[hbm] * 5,
        scratch_shapes=[pltpu.SemaphoreType.DMA((5,))],
        compiler_params=pltpu.CompilerParams(vmem_limit_bytes=2**20),
    )(held)


def solution(mesh):
    four = P(("pole", "row"), None, None, None)
    three = P(("pole", "row"), None, None)
    two = P(("pole", "row"), None)
    return jax.shard_map(
        body,
        mesh=mesh,
        in_specs=(four, four, two, three, four, two, three, three),
        out_specs=(four, three, four, three, three),
        check_vma=False,
    )
```

```python
import functools

import jax
import jax.numpy as jnp
from jax import lax
from jax.experimental import pallas as pl
from jax.experimental.pallas import tpu as pltpu
from jax.sharding import PartitionSpec as P

TILE = 256
DETOURS = {3: 112, 7: 80, 11: 48, 5: 80, 9: 48}
MESH = pl.DeviceIdType.MESH


def columns(block):
    def wrap(step):
        @pl.loop(0, block // TILE)
        def _(c):
            step(pl.ds(pl.multiple_of(c * TILE, TILE), TILE))

    return wrap


def plain(left, right):
    return jnp.dot(left[...], right, preferred_element_type=jnp.float32)


def turned(left, right):
    return lax.dot_general(
        left[...], right, (((0,), (0,)), ((), ())), preferred_element_type=jnp.float32
    )


def kernel(
    count,
    mask_one, mask_two, anc, p_one, d_one, p_two, par_in, d_two,
    out,
    a, one, two, par, dinv_one, dinv_two,
    near, far, got_one, got_two, inv_one, inv_two,
    diag_one, cross, diag_two, part_one, part_two, m_one, m_two, flags, got_flags, via,
    load_sem, store_sem, send_sem, recv_sem, go_sem,
):
    block = par.shape[0]
    me = lax.axis_index("row")
    odd = lax.rem(me, 2) == 1
    upper = lax.rem(me, 4) >= 2
    lower = jnp.logical_not(upper)
    last = me >= count - 2
    def at(places):
        return functools.reduce(jnp.logical_or, [me == count - i for i in places])

    asides = {
        size: [i for i in DETOURS if DETOURS[i] == size] for size in sorted(set(DETOURS.values()))
    }
    sends_aside = at(DETOURS)
    bounds = (0, block // 8, block // 2, block)
    pieces = [pl.ds(a, b - a) for a, b in zip(bounds, bounds[1:])]
    up = [None] + [lax.rem(me + q, count) for q in (1, 2)]
    down = [None] + [lax.rem(me + count - q, count) for q in (1, 2)]

    loads = [
        pltpu.make_async_copy(source, target, load_sem.at[i])
        for i, (source, target) in enumerate(
            [
                (mask_one, m_one),
                (mask_two, m_two),
                (p_one.at[0, 0], one),
                (anc.at[0], a),
                (p_two.at[0, 0], two),
                (par_in.at[0], par),
                (d_one.at[0], dinv_one),
                (d_two.at[0], dinv_two),
            ]
        )
    ]
    barrier = pltpu.get_barrier_semaphore()
    for peer in up[1:]:
        pl.semaphore_signal(barrier, inc=1, device_id={"row": peer}, device_id_type=MESH)
    for load in loads:
        load.start()
    pl.semaphore_wait(barrier, 2)

    def remote(source, target, send, recv, peer):
        return pltpu.make_async_remote_copy(
            src_ref=source,
            dst_ref=target,
            send_sem=send_sem.at[send],
            recv_sem=recv_sem.at[recv],
            device_id={"row": peer},
            device_id_type=MESH,
        )

    near_0 = remote(anc.at[0, 0], near.at[0], 0, 0, down[1])
    near_1 = remote(anc.at[0, 1], near.at[1], 1, 1, down[1])
    far_odd = remote(anc.at[0, 0], far, 2, 2, down[2])
    far_pass = remote(near.at[0], far, 7, 2, down[1])
    send_one = [None] + [remote(p_one.at[0, q], got_one.at[q - 1], 2 + q, 2 + q, down[q]) for q in (1, 2)]
    send_two = [None] + [remote(p_two.at[0, q], got_two.at[q - 1], 4 + q, 4 + q, down[q]) for q in (1, 2)]
    send_two = send_two[2:] + [
        remote(p_two.at[0, 1, piece], got_two.at[0, piece], 14 + i, 13 + i, down[1])
        for i, piece in enumerate(pieces)
    ]
    send_flags = [None] + [remote(flags, got_flags.at[q - 1], 7 + q, 6 + q, down[q]) for q in (1, 2)]
    give_one = [None] + [remote(inv_one.at[p], out.at[p], 9 + p, 8 + p, up[p]) for p in (1, 2)]
    def part(size):
        rest = pl.ds(size, block - size)
        return remote(inv_one.at[2, rest], out.at[2, rest], 11, 10, up[2])

    def detour(size):
        aside = pl.ds(0, size)
        return remote(inv_one.at[2, aside], via.at[aside], 17, 16, down[2])

    def onward(size):
        aside = pl.ds(0, size)
        return remote(via.at[aside], out.at[2, aside], 18, 17, lax.rem(me + 4, count))

    def by_size(shift, act):
        for size, places in asides.items():
            @pl.when(at([i + shift for i in places]))
            def _():
                act(size)

    give_two = [None] + [remote(inv_two.at[p], out.at[3 + p], 11 + p, 10 + p, up[p]) for p in (1, 2)]

    near_0.start()
    loads[0].wait()
    loads[1].wait()
    flag_one = [None] + [m_one[0, q].astype(jnp.float32) for q in (1, 2)]
    flag_two = [None] + [flag_one[q] * m_two[0, q].astype(jnp.float32) for q in (1, 2)]
    spot = lax.broadcasted_iota(jnp.int32, flags.shape, 0)
    value = jnp.where(spot == 0, flag_one[1], flag_one[2])
    value = jnp.where(spot == 2, flag_two[1], value)
    flags[...] = jnp.where(spot == 3, flag_two[2], value)
    for q in (2, 1):
        send_flags[q].start()
    send_one[2].start()
    send_one[1].start()
    near_1.start()

    @pl.when(odd)
    def _():
        far_odd.start()

    for copy in send_two:
        copy.start()

    def kept(p, level):
        return got_flags[p - 1, pl.ds(2 * level + p - 1, 1), 0:1]

    def masked(ref, q, level):
        flag = kept(q, level).astype(ref.dtype)

        @pl.loop(0, block // 64)
        def _(r):
            rows = pl.ds(pl.multiple_of(r * 64, 64), 64)
            ref[rows, :] = ref[rows, :] * flag

    for load in loads[2:]:
        load.wait()

    @columns(block)
    def _(c):
        for part, own in ((part_one, one), (part_two, two)):
            part[0, :, c] = plain(a.at[0], own[:, c])
            for p in (1, 2):
                part[p, :, c] = turned(a.at[p], own[:, c])

    near_0.wait_recv()

    @pl.when(jnp.logical_not(odd))
    def _():
        far_odd.wait_recv()

    @pl.when(odd)
    def _():
        far_pass.start()

    for q in (1, 2):
        send_flags[q].wait_recv()

    for q in (1, 2):
        send_one[q].wait_recv()
        masked(got_one.at[q - 1], q, 0)

    def solve(p, c, got, total):
        first, second = got[0, :, c], got[1, :, c]
        if p == 0:
            return total + plain(a.at[1], first) + plain(a.at[2], second)
        if p == 1:
            return total + plain(near.at[0], first) + plain(near.at[1], second)
        return total + turned(near.at[1], first) + plain(far, second)

    def give_far():
        by_size(0, lambda size: part(size).start())

        @pl.when(jnp.logical_not(sends_aside))
        def _():
            give_one[2].start()

    def negated(p, level, total):
        return -total * kept(p, level) if p else -total

    near_1.wait_recv()

    @pl.when(odd)
    def _():
        far_odd.wait_recv()

    for p in (2, 1, 0):
        @columns(block)
        def _(c):
            total = solve(p, c, got_one, part_one[p, :, c])
            inv_one[p, :, c] = negated(p, 0, total).astype(jnp.bfloat16)

        if p == 2:
            by_size(0, lambda size: detour(size).start())

            @pl.when(lower | last)
            def _():
                give_far()

        if p == 1:
            @pl.when(lower)
            def _():
                give_one[1].start()

    stores = []

    def store(source, target):
        stores.append(pltpu.make_async_copy(source, target, store_sem.at[len(stores)]))
        stores[-1].start()

    store(inv_one.at[0], out.at[0])

    for p in (2, 1, 0):
        @columns(block)
        def _(c):
            part_two[p, :, c] += plain(inv_one.at[p], par[:, c])

    @columns(block)
    def _(c):
        total = dinv_one[:, c].astype(jnp.float32) - turned(one, inv_one[0, :, c])
        for q in (1, 2):
            total = total - turned(got_one.at[q - 1], inv_one[q, :, c])
        diag_one[:, c] = total.astype(jnp.bfloat16)

    store(diag_one, out.at[6])

    @pl.when(upper)
    def _():
        pl.semaphore_wait(go_sem, 1)

        @pl.when(jnp.logical_not(last))
        def _():
            give_far()

        @pl.when(odd)
        def _():
            pl.semaphore_signal(go_sem, inc=1, device_id={"row": down[1]}, device_id_type=MESH)

        give_one[1].start()

    def let_go(here):
        @pl.when(here)
        def _():
            pl.semaphore_signal(go_sem, inc=1, device_id={"row": down[2]}, device_id_type=MESH)

    wrap = me == 1
    send_two[1].wait_recv()
    let_go(wrap)
    send_two[2].wait_recv()
    let_go(lower & odd & jnp.logical_not(wrap))
    send_two[0].wait_recv()
    masked(got_two.at[1], 2, 1)
    send_two[3].wait_recv()
    masked(got_two.at[0], 1, 1)
    for p in (1, 2, 0):
        @columns(block)
        def _(c):
            total = solve(p, c, got_two, part_two[p, :, c])
            inv_two[p, :, c] = negated(p, 1, total).astype(jnp.bfloat16)

        if p:
            give_two[p].start()

    store(inv_two.at[0], out.at[3])

    def pass_on(size):
        detour(size).wait_recv()
        onward(size).start()

    by_size(2, pass_on)

    @columns(block)
    def _(c):
        total = plain(diag_one, par[:, c]) + turned(inv_one.at[0], two[:, c])
        for q in (1, 2):
            total = total + turned(inv_one.at[q], got_two[q - 1, :, c])
        cross[:, c] = (-total).astype(jnp.bfloat16)

    store(cross, out.at[7])

    @columns(block)
    def _(c):
        total = dinv_two[:, c].astype(jnp.float32) - turned(par, cross[:, c])
        total = total - turned(two, inv_two[0, :, c])
        for q in (1, 2):
            total = total - turned(got_two.at[q - 1], inv_two[q, :, c])
        diag_two[:, c] = total.astype(jnp.bfloat16)

    store(diag_two, out.at[8])

    @pl.when(odd)
    def _():
        far_pass.wait_send()

    @pl.when(odd)
    def _():
        far_odd.wait_send()

    for copy in [near_0, near_1] + send_two:
        copy.wait_send()
    for group in (send_flags, send_one, give_two):
        for q in (1, 2):
            group[q].wait_send()
    give_one[1].wait_send()

    def aside_sent(size):
        part(size).wait_send()
        detour(size).wait_send()

    by_size(0, aside_sent)

    @pl.when(jnp.logical_not(sends_aside))
    def _():
        give_one[2].wait_send()

    for item in stores:
        item.wait()

    def aside_here(size):
        part(size).wait_recv()
        onward(size).wait_recv()

    by_size(-2, aside_here)

    @pl.when(jnp.logical_not(at([i - 2 for i in DETOURS])))
    def _():
        give_one[2].wait_recv()

    by_size(2, lambda size: onward(size).wait_send())

    for give in (give_one[1], give_two[1], give_two[2]):
        give.wait_recv()


def place(held, o_inv_one, o_diag_one, o_inv_two, o_cross, o_diag_two, sem):
    copies = [
        pltpu.make_async_copy(source, target, sem.at[i])
        for i, (source, target) in enumerate(
            [
                (held.at[pl.ds(0, 3)], o_inv_one.at[0]),
                (held.at[pl.ds(3, 3)], o_inv_two.at[0]),
                (held.at[6], o_diag_one.at[0]),
                (held.at[7], o_cross.at[0]),
                (held.at[8], o_diag_two.at[0]),
            ]
        )
    ]
    for copy in copies:
        copy.start()
    for copy in copies:
        copy.wait()


def body(anc_band, panel_one, mask_one, dinv_one, panel_two, mask_two, par_two, dinv_two):
    block = anc_band.shape[2]
    kind = anc_band.dtype

    def blocks(number, dtype=kind):
        lead = () if number is None else (number,)
        return pltpu.VMEM(lead + (block, block), dtype)

    hbm = pl.BlockSpec(memory_space=pltpu.HBM)
    free = pl.BlockSpec(memory_space=pl.ANY)
    count = lax.axis_size("row")
    held = pl.pallas_call(
        functools.partial(kernel, count),
        out_shape=pltpu.VMEM((9, block, block), kind),
        in_specs=[hbm] * 8,
        out_specs=free,
        scratch_shapes=[
            blocks(3), blocks(None), blocks(None), blocks(None), blocks(None), blocks(None),
            blocks(2), blocks(None), blocks(2), blocks(2), blocks(3), blocks(3),
            blocks(None), blocks(None), blocks(None), blocks(3, jnp.float32), blocks(3, jnp.float32),
            pltpu.SMEM(mask_one.shape, jnp.int32), pltpu.SMEM(mask_two.shape, jnp.int32),
            pltpu.VMEM((8, 128), jnp.float32), pltpu.VMEM((2, 8, 128), jnp.float32), pltpu.VMEM((max(DETOURS.values()), block), kind),
            pltpu.SemaphoreType.DMA((8,)),
            pltpu.SemaphoreType.DMA((5,)),
            pltpu.SemaphoreType.DMA((19,)),
            pltpu.SemaphoreType.DMA((18,)),
            pltpu.SemaphoreType.REGULAR,
        ],
        compiler_params=pltpu.CompilerParams(
            collective_id=0, has_side_effects=True, vmem_limit_bytes=40 * 2**20
        ),
    )(*(
        pltpu.with_memory_space_constraint(x, pltpu.HBM)
        for x in (mask_one, mask_two, anc_band, panel_one, dinv_one, panel_two, par_two, dinv_two)
    ))
    return pl.pallas_call(
        place,
        out_shape=[
            jax.ShapeDtypeStruct(anc_band.shape, kind),
            jax.ShapeDtypeStruct(dinv_one.shape, kind),
            jax.ShapeDtypeStruct(anc_band.shape, kind),
            jax.ShapeDtypeStruct(dinv_one.shape, kind),
            jax.ShapeDtypeStruct(dinv_one.shape, kind),
        ],
        in_specs=[free],
        out_specs=[hbm] * 5,
        scratch_shapes=[pltpu.SemaphoreType.DMA((5,))],
        compiler_params=pltpu.CompilerParams(vmem_limit_bytes=2**20),
    )(held)


def solution(mesh):
    four = P(("pole", "row"), None, None, None)
    three = P(("pole", "row"), None, None)
    two = P(("pole", "row"), None)
    return jax.shard_map(
        body,
        mesh=mesh,
        in_specs=(four, four, two, three, four, two, three, three),
        out_specs=(four, three, four, three, three),
        check_vma=False,
    )
```
